512 devices in a mesh: dp: 128 (over z, y, core), mp: 4 (over x).
Axes of the slice: x: 4, y: 8, z: 8, core: 2. Of those that a mesh axis runs over, the one named last changes fastest.
Arguments:
- hot_ids: int32 [131072, 7], P('dp'), may hold values from 0 to 1023
- touched: int32 [128, 4, 256], P('dp', 'mp'), may hold values from 0 to 131071, as said below
- cold_items: int32 [128, 4, 2048], P('dp', 'mp'), may hold values from 0 to 255
- bag_counts: int32 [128, 4, 1024], P('dp', 'mp'), may hold values from 1 to 8, 2048 in all within a row
- owner_map: int32 [131072], replicated, may hold values from 0 to 131071, as said below
- grad_out: bfloat16 [131072, 256], P('dp'), may hold values from -6 to 6
- weight_in: bfloat16 [1024, 512], P(None, 'mp'), may hold values from -0.1875 to 0.1875
- bias_in: float32 [512], P('mp'), may hold values from -4 to 4
- weight_out: bfloat16 [512, 256], P('mp'), may hold values from -0.25 to 0.25
- hot_table: float32 [1024, 128], replicated, may hold values from -6 to 6
- hot_accum: float32 [1024, 128], replicated, may hold values from 0.25 to 4
- cold_table: float32 [131072, 128], P(('dp', 'mp')), may hold values from -6 to 6
- cold_accum: float32 [131072, 128], P(('dp', 'mp')), may hold values from 0.25 to 4
Outputs:
- hot_updated: float32 [1024, 128], replicated
- hot_accum_new: float32 [1024, 128], replicated
- cold_updated: float32 [131072, 128], P(('dp', 'mp'))
- cold_accum_new: float32 [131072, 128], P(('dp', 'mp'))
The draws below stay inside these ranges and needn't reach their ends.
Inputs may be any that keep to these rules, and one draw needn't show every extreme that they name: owner_map is a permutation of the cold row ids: cold row g is stored in row owner_map[g] of cold_table. `touched`: the 256 ids of one device are distinct, and owner_map sends all of them to rows stored on devices with the same mp index as that device; at most 4 of them are stored on any one dp index, and exactly 4 on some.
All inputs are finite; a program needn't handle non-finite values.
Results may differ from the reference program's by a relative error of at most 0.0038.
Values may be sent and summed in bfloat16 or wider, within the bound.
A program may use at most 64 MiB of HBM per device.

```python
import math
import jax
import jax.numpy as jnp
import numpy as np
from jax import lax

E = 128
HOTF = 7
D_IN = 1024
H1 = 512
H2 = 256
B = 1024
HOT = 1024
SLOTS = 256
TOUCH = 256
MOSTBAG = 8
ITEMS = 2048
COLD = 131072
N_DP = 128
N_MP = 4


def storage_order(key):
    return jax.random.permutation(jax.random.fold_in(key, 11), COLD).astype(jnp.int32)


def draw_owner_map(key, part):
    return storage_order(key)


def draw_touched(key, part):
    placed = storage_order(key)
    inverse = jnp.zeros((COLD,), jnp.int32).at[placed].set(jnp.arange(COLD, dtype=jnp.int32))
    hot_count = max(1, N_DP // 16)
    capacity = 2 * TOUCH // N_DP
    rest_count = TOUCH - hot_count * capacity
    other_count = N_DP - hot_count
    base_count = rest_count // other_count
    extra_count = rest_count - base_count * other_count
    owner_iota = jnp.arange(N_DP, dtype=jnp.int32)
    scores = jax.random.randint(jax.random.fold_in(key, 21), (N_MP, N_DP), 0, 1 << 20, dtype=jnp.int32) * N_DP + owner_iota
    rank_of = jnp.argsort(jnp.argsort(scores, axis=1), axis=1).astype(jnp.int32)
    is_hot = (rank_of < hot_count).astype(jnp.int32)
    extra_scores = jax.random.randint(jax.random.fold_in(key, 22), (N_DP, N_MP, N_DP), 0, 1 << 20, dtype=jnp.int32) * N_DP + owner_iota + is_hot[None, :, :] * (1 << 30)
    extra_rank = jnp.argsort(jnp.argsort(extra_scores, axis=2), axis=2).astype(jnp.int32)
    gets_extra = (extra_rank < extra_count).astype(jnp.int32)
    counts = jnp.where(is_hot[None, :, :] == 1, capacity, base_count + gets_extra).astype(jnp.int32)
    end_pos = jnp.cumsum(counts, axis=2).astype(jnp.int32)
    offsets = (end_pos - counts).astype(jnp.int32)
    touch_iota = jnp.arange(TOUCH, dtype=jnp.int32)
    owner_of = jax.vmap(lambda ends: jnp.searchsorted(ends, touch_iota, side='right'))(end_pos.reshape(-1, N_DP)).astype(jnp.int32).reshape(N_DP, N_MP, TOUCH)
    within = touch_iota[None, None, :] - jnp.take_along_axis(offsets, owner_of, axis=2)
    start_slot = jax.random.randint(jax.random.fold_in(key, 23), (N_DP, N_MP, N_DP), 0, SLOTS, dtype=jnp.int32)
    slot_of = (jnp.take_along_axis(start_slot, owner_of, axis=2) + within) % SLOTS
    mp_iota = jnp.arange(N_MP, dtype=jnp.int32)
    position = (owner_of * N_MP + mp_iota[None, :, None]) * SLOTS + slot_of
    ids_sorted = inverse[position]
    shuffle_scores = jax.random.randint(jax.random.fold_in(key, 24), (N_DP, N_MP, TOUCH), 0, 1 << 20, dtype=jnp.int32) * TOUCH + touch_iota
    order_idx = jnp.argsort(shuffle_scores, axis=2).astype(jnp.int32)
    return jnp.take_along_axis(ids_sorted, order_idx, axis=2).astype(jnp.int32)


def touch_ends(result, stream_key, low, top_value):
    index_at = [jax.random.randint(jax.random.fold_in(stream_key, axis), (), 0, length) for axis, length in enumerate(result.shape)]
    longest = result.shape.index(max(result.shape))
    beside = index_at[:longest] + [(index_at[longest] + 1) % result.shape[longest]] + index_at[longest + 1:]
    return result.at[tuple(index_at)].set(low).at[tuple(beside)].set(top_value)


def level_of(rng, dims, cuts, low, largest):
    def one(dim, blocks):
        draws = jax.random.uniform(jax.random.fold_in(jax.random.fold_in(rng, 6), dim), (blocks,), jnp.float32, low / len(cuts), largest / len(cuts))
        return jnp.repeat(jnp.exp(draws), dims[dim] // blocks).reshape((-1,) + (1,) * (len(dims) - dim - 1))

    gain = one(*cuts[0])
    for cut in cuts[1:]:
        gain = gain * one(*cut)
    return gain


def rank_table(number_of, lean):
    portions = [(1 << 20) // math.isqrt(standing ** lean) + 1 for standing in range(1, number_of + 1)]
    deviation = 1 + sum(portions) // (1 << 30)
    return np.cumsum(np.array([max(1, weight // deviation) for weight in portions]))


def ranked(key, extent, count, slope):
    grid = rank_table(count, slope)
    lot = jax.random.randint(jax.random.fold_in(key, 1), extent, 0, int(grid[count - 1]))
    rank = jnp.searchsorted(jnp.asarray(grid, jnp.int32), lot, side="right")
    return jax.random.permutation(jax.random.fold_in(key, 2), count)[rank].astype(jnp.int32)


def length_profile(amount, total, bound, skew):
    portions = [(1 << 20) // math.isqrt(rank ** skew) + 1 for rank in range(2, amount + 1)]
    spare, given = total - bound - (amount - 1), [1] * (amount - 1)
    while spare > 0:
        movable = [i for i in range(amount - 1) if given[i] < bound]
        mass, left = sum([portions[i] for i in movable]), spare
        for i in movable:
            addition = min(bound - given[i], max(1, left * portions[i] // mass), spare)
            given[i] = given[i] + addition
            spare = spare - addition
    return np.array([bound] + given)


def uneven(key, number_of, total, bound, skew):
    if number_of == 2:
        one = jax.random.randint(key, (), max(1, total - bound), min(bound, total - 1) + 1)
        return jnp.stack([one, total - one])
    sizes = jnp.asarray(length_profile(number_of, total, bound, skew), jnp.int32)
    twos = (number_of - 1) // 2
    donor, taker = sizes[1:1 + 2 * twos:2], sizes[2:2 + 2 * twos:2]
    room = jnp.minimum(donor - 1, bound - taker)
    passed = jax.random.randint(jax.random.fold_in(key, 1), (twos,), 0, 1 << 20) % (room + 1)
    sizes = sizes.at[1:1 + 2 * twos:2].set(donor - passed).at[2:2 + 2 * twos:2].set(taker + passed)
    return sizes[jax.random.permutation(jax.random.fold_in(key, 2), number_of)]


def gaussian(rng, dims, width, bound, pieces=(), kind=jnp.bfloat16):
    result = width * jax.random.normal(rng, dims, jnp.float32)
    if pieces:
        result = result * level_of(rng, dims, pieces, -0.22, 0.18)
    return jnp.clip(result, -bound, bound).astype(kind)


def setup_inputs(seed: int = 0) -> dict:
    key_list = jax.random.split(jax.random.key(seed), 14)
    return {
        "hot_ids": touch_ends(ranked(key_list[0], (N_DP * B, HOTF), HOT, 2), jax.random.fold_in(key_list[0], 3), 0, HOT - 1).astype(jnp.int32),
        "touched": draw_touched(jax.random.fold_in(key_list[13], 71), 0),
        "cold_items": touch_ends(jax.random.randint(key_list[2], (N_DP, N_MP, ITEMS), 0, TOUCH), jax.random.fold_in(key_list[2], 1), 0, TOUCH - 1).astype(jnp.int32),
        "bag_counts": jax.vmap(lambda own: uneven(own, B, ITEMS, MOSTBAG, 2))(jax.random.split(key_list[3], N_DP * N_MP)).reshape((N_DP, N_MP, B)).astype(jnp.int32),
        "owner_map": draw_owner_map(jax.random.fold_in(key_list[13], 71), 0),
        "grad_out": gaussian(key_list[5], (N_DP * B, H2), 1.0, 6.0, ((0, 128),)),
        "weight_in": gaussian(key_list[6], (D_IN, H1), D_IN ** -0.5, 0.1875, ((1, 4),)),
        "bias_in": gaussian(key_list[7], (H1,), 1.0, 4.0, ((0, 4),), jnp.float32),
        "weight_out": gaussian(key_list[8], (H1, H2), H1 ** -0.5, 0.25, ((0, 4),)),
        "hot_table": gaussian(key_list[9], (HOT, E), 1.0, 6.0, (), jnp.float32),
        "hot_accum": jnp.clip(jnp.exp(jax.random.uniform(key_list[10], (HOT, E), jnp.float32, math.log(0.25), math.log(4.0))), 0.25, 4.0),
        "cold_table": gaussian(key_list[11], (COLD, E), 1.0, 6.0, ((0, 512),), jnp.float32),
        "cold_accum": jnp.clip(jnp.exp(math.log(4.0) - 2.7725887 * jax.random.uniform(key_list[12], (COLD, E), jnp.float32) ** level_of(key_list[12], (COLD, E), ((0, 512),), -0.2, 0.2)), 0.25, 4.0),
    }


STEP_SIZE = 0.5
HIGHEST = lax.Precision.HIGHEST

def adagrad(table_rows, accum_rows, grad_rows):
    accum_new = accum_rows + grad_rows * grad_rows
    return (table_rows - STEP_SIZE * grad_rows / jnp.sqrt(accum_new), accum_new)

def reference(hot_ids, touched, cold_items, bag_counts, owner_map, grad_out, weight_in, bias_in, weight_out, hot_table, hot_accum, cold_table, cold_accum):
    dp_count = touched.shape[0]
    hot_cols = HOTF * E
    ids_grouped = hot_ids.reshape(dp_count, B, HOTF)
    grads_grouped = grad_out.reshape(dp_count, B, H2)
    item_pos = jnp.arange(ITEMS, dtype=jnp.int32)
    touch_pos = jnp.arange(TOUCH, dtype=jnp.int32)

    def per_group(group_args):
        group_ids, group_grads, group_touched, group_items, group_counts = group_args
        stored_at = owner_map[group_touched]
        fetched = cold_table[stored_at]
        end_pos = jnp.cumsum(group_counts, axis=1).astype(jnp.int32)
        start_pos = (end_pos - group_counts).astype(jnp.int32)
        member = ((item_pos[None, None, :] >= start_pos[:, :, None]) & (item_pos[None, None, :] < end_pos[:, :, None])).astype(jnp.float32)
        picks = (group_items[:, :, None] == touch_pos[None, None, :]).astype(jnp.float32)
        count_mat = jnp.einsum('mbi,mit->mbt', member, picks, precision=HIGHEST)
        pooled = jnp.einsum('mbt,mte->be', count_mat, fetched, precision=HIGHEST)
        hot_rows = hot_table[group_ids].reshape(B, hot_cols)
        inputs = jnp.concatenate([hot_rows, pooled], axis=1).astype(jnp.bfloat16)
        pre_act = jnp.dot(inputs, weight_in, preferred_element_type=jnp.float32) + bias_in
        back_grad = jnp.dot(group_grads, weight_out.T, preferred_element_type=jnp.float32)
        sigmoid_val = jax.nn.sigmoid(pre_act)
        hidden_grad = (back_grad * sigmoid_val * (1.0 + pre_act * (1.0 - sigmoid_val))).astype(jnp.bfloat16)
        input_grad = jnp.dot(hidden_grad, weight_in.T, preferred_element_type=jnp.float32)
        hot_part = jax.ops.segment_sum(input_grad[:, :hot_cols].reshape(B * HOTF, E), group_ids.reshape(B * HOTF), num_segments=HOT)
        touch_grad = jnp.einsum('mbt,be->mte', count_mat, input_grad[:, hot_cols:], precision=HIGHEST)
        return (hot_part, stored_at.reshape(-1), touch_grad.reshape(-1, E))
    hot_parts, positions, touch_grads = lax.map(per_group, (ids_grouped, grads_grouped, touched, cold_items, bag_counts))
    hot_grad = lax.optimization_barrier(jnp.sum(hot_parts, axis=0))
    cold_grad = jax.ops.segment_sum(touch_grads.reshape(-1, E), positions.reshape(-1), num_segments=COLD)
    hot_updated, hot_accum_new = adagrad(hot_table, hot_accum, hot_grad)
    cold_updated, cold_accum_new = adagrad(cold_table, cold_accum, cold_grad)
    return (hot_updated, hot_accum_new, cold_updated, cold_accum_new)
```

```python
import functools

import jax
import jax.numpy as jnp
from jax import lax
from jax.experimental import pallas as pl
from jax.experimental.pallas import tpu as pltpu
from jax.sharding import PartitionSpec as P

STEP_SIZE = 0.5
HIGHEST = lax.Precision.HIGHEST

MESH = pl.DeviceIdType.MESH
NY, NZ = 8, 8

def coords():
    dp, mp = lax.axis_index("dp"), lax.axis_index("mp")
    return dp // 16, (dp // 2) % 8, dp % 2, mp

def dev(z, y, c, x):
    return (z * 16 + y * 2 + c, x)

def hot_allreduce_kernel(part, full, r_core, a_half, r_x, a_x, r_z, b_y, snd, rcv):
    z, y, c, x = coords()
    barrier = pltpu.get_barrier_semaphore()
    peers = [dev(z, y, 1 - c, x)]
    peers += [dev(z, y, c, (x + o) % 4) for o in range(1, 4)]
    peers += [dev((z + o) % 8, y, c, x) for o in range(1, 8)]
    peers += [dev(z, (y + o) % 8, c, x) for o in range(1, 8)]
    for p in peers:
        pl.semaphore_signal(barrier, inc=1, device_id=p, device_id_type=MESH)
    pl.semaphore_wait(barrier, len(peers))
    n = [0]
    def copy(src, dst, to):
        k = n[0]; n[0] += 1
        cp = pltpu.make_async_remote_copy(src_ref=src, dst_ref=dst, send_sem=snd.at[k], recv_sem=rcv.at[k],
                                          device_id=to, device_id_type=MESH)
        cp.start()
        return cp
    sends = []
    other = pl.multiple_of((1 - c) * 512, 512)
    mine = pl.multiple_of(c * 512, 512)
    cp = copy(part.at[pl.ds(other, 512)], r_core, dev(z, y, 1 - c, x))
    cp.wait_recv(); sends.append(cp)
    a_half[...] = part[pl.ds(mine, 512)] + r_core[...]
    cps = []
    for o in range(1, 4):
        xo = (x + o) % 4
        cps.append(copy(a_half.at[pl.ds(pl.multiple_of(xo * 128, 128), 128)], r_x.at[o - 1], dev(z, y, c, xo)))
    for cp in cps: cp.wait_recv()
    sends += cps
    a_x[...] = a_half[pl.ds(pl.multiple_of(x * 128, 128), 128)] + r_x[0] + r_x[1] + r_x[2]
    cps = []
    for o in range(1, 8):
        zo = (z + o) % 8
        cps.append(copy(a_x.at[pl.ds(pl.multiple_of(zo * 16, 16), 16)], r_z.at[o - 1], dev(zo, y, c, x)))
    for cp in cps: cp.wait_recv()
    sends += cps
    s = a_x[pl.ds(pl.multiple_of(z * 16, 16), 16)]
    for o in range(7): s += r_z[o]
    b_y[y] = s
    cps = []
    for o in range(1, 8):
        yo = (y + o) % 8
        cps.append(copy(b_y.at[y], b_y.at[y], dev(z, yo, c, x)))
    for cp in cps: cp.wait_recv()
    sends += cps
    s = b_y[0]
    for o in range(1, 8): s += b_y[o]
    own = pl.ds(pl.multiple_of(c * 512 + x * 128 + z * 16, 16), 16)
    full[own] = s
    cps = []
    for o in range(1, 8):
        cps.append(copy(full.at[own], full.at[own], dev((z + o) % 8, y, c, x)))
    for cp in cps: cp.wait_recv()
    sends += cps
    own = pl.ds(pl.multiple_of(c * 512 + x * 128, 128), 128)
    cps = []
    for o in range(1, 4):
        cps.append(copy(full.at[own], full.at[own], dev(z, y, c, (x + o) % 4)))
    sends += cps
    fw = [copy(full.at[own], full.at[own], dev(z, y, 1 - c, x))]
    for o, cp in zip(range(1, 4), cps):
        cp.wait_recv()
        blk = pl.ds(pl.multiple_of(c * 512 + ((x + 4 - o) % 4) * 128, 128), 128)
        fw.append(copy(full.at[blk], full.at[blk], dev(z, y, 1 - c, x)))
    for cp in fw: cp.wait_recv()
    sends += fw
    for cp in sends: cp.wait_send()

def hot_allreduce(part, cid=0):
    f = jnp.float32
    ncp = 1 + 3 + 7 + 7 + 7 + 3 + 4
    return pl.pallas_call(
        hot_allreduce_kernel,
        out_shape=jax.ShapeDtypeStruct((1024, 128), f),
        in_specs=[pl.BlockSpec(memory_space=pltpu.VMEM)],
        out_specs=pl.BlockSpec(memory_space=pltpu.VMEM),
        scratch_shapes=[pltpu.VMEM((512, 128), f), pltpu.VMEM((512, 128), f), pltpu.VMEM((3, 128, 128), f),
                        pltpu.VMEM((128, 128), f), pltpu.VMEM((7, 16, 128), f), pltpu.VMEM((8, 16, 128), f),
                        pltpu.SemaphoreType.DMA((ncp,)), pltpu.SemaphoreType.DMA((ncp,))],
        compiler_params=pltpu.CompilerParams(collective_id=cid, has_side_effects=True, vmem_limit_bytes=32 << 20),
    )(part)


def exchange_kernel(x_ref, o_ref, snd, rcv):
    dp, mp = lax.axis_index("dp"), lax.axis_index("mp")
    barrier = pltpu.get_barrier_semaphore()

    @pl.loop(1, 128)
    def _(o):
        pl.semaphore_signal(barrier, inc=1, device_id=((dp + o) % 128, mp), device_id_type=MESH)

    pl.semaphore_wait(barrier, 127)

    @pl.loop(1, 128)
    def _(o):
        to = (dp + o) % 128
        pltpu.make_async_remote_copy(
            src_ref=x_ref.at[to], dst_ref=o_ref.at[dp], send_sem=snd, recv_sem=rcv,
            device_id=(to, mp), device_id_type=MESH,
        ).start()

    o_ref[dp] = x_ref[dp]
    pltpu.make_async_copy(o_ref.at[pl.ds(0, 127)], o_ref.at[pl.ds(0, 127)], rcv).wait()
    pltpu.make_async_copy(x_ref.at[pl.ds(0, 127)], x_ref.at[pl.ds(0, 127)], snd).wait()


def exchange(x, cid):
    vmem = pl.BlockSpec(memory_space=pltpu.VMEM)
    return pl.pallas_call(
        exchange_kernel,
        out_shape=jax.ShapeDtypeStruct(x.shape, x.dtype),
        in_specs=[vmem],
        out_specs=vmem,
        scratch_shapes=[pltpu.SemaphoreType.DMA, pltpu.SemaphoreType.DMA],
        compiler_params=pltpu.CompilerParams(collective_id=cid, has_side_effects=True),
    )(x)


def adagrad(table_rows, accum_rows, grad_rows):
    accum_new = accum_rows + grad_rows * grad_rows
    return (table_rows - STEP_SIZE * grad_rows / jnp.sqrt(accum_new), accum_new)


def silu_grad(pre_act, back_grad):
    sigmoid_val = jax.nn.sigmoid(pre_act)
    return (back_grad * sigmoid_val * (1.0 + pre_act * (1.0 - sigmoid_val))).astype(jnp.bfloat16)


def per_device(
    hot_ids,
    touched,
    cold_items,
    bag_counts,
    owner_map,
    grad_out,
    weight_in,
    bias_in,
    weight_out,
    hot_table,
    hot_accum,
    cold_table,
    cold_accum,
):
    dp_count = lax.axis_size("dp")
    mp_count = lax.axis_size("mp")
    slot_count = cold_table.shape[0]
    emb_width = cold_table.shape[1]
    samples = hot_ids.shape[0]
    fields = hot_ids.shape[1]
    hot_cols = fields * emb_width
    touch_count = touched.shape[2]
    capacity = 2 * touch_count // dp_count
    share_rows = samples // mp_count
    my_start = lax.axis_index("mp") * share_rows
    my_ids = touched[0, 0]
    stored_at = owner_map[my_ids]
    owner_dp = stored_at // (mp_count * slot_count)
    slot_index = stored_at % slot_count
    owner_hits = (owner_dp[:, None] == jnp.arange(dp_count, dtype=jnp.int32)[None, :]).astype(
        jnp.float32
    )
    touch_iota = jnp.arange(touch_count, dtype=jnp.int32)
    earlier = (touch_iota[:, None] > touch_iota[None, :]).astype(jnp.float32)
    before_mine = jnp.dot(earlier, owner_hits, precision=HIGHEST)
    rank_owner = jnp.sum(before_mine * owner_hits, axis=1).astype(jnp.int32)
    bucket_pos = owner_dp * capacity + rank_owner
    requests = (
        jnp.zeros((dp_count * capacity,), jnp.int32)
        .at[bucket_pos]
        .set(slot_index)
        .reshape(dp_count, capacity)
    )
    padded = jnp.pad(requests, ((0, 0), (0, 124))).reshape(dp_count, 1, 128)
    asked_slots = exchange(padded, 1)[:, 0, :capacity]
    rows_out = cold_table[asked_slots]
    rows_back = exchange(rows_out, 2)
    fetched = rows_back.reshape(dp_count * capacity, emb_width)[bucket_pos]
    bag_sizes = bag_counts[0, 0]
    upto = (jnp.arange(samples)[:, None] >= jnp.arange(samples)[None, :]).astype(jnp.bfloat16)
    end_pos = jnp.dot(upto, bag_sizes.astype(jnp.bfloat16), preferred_element_type=jnp.float32).astype(jnp.int32)
    start_pos = end_pos - bag_sizes
    items_here = cold_items[0, 0]
    item_pos = jnp.arange(items_here.shape[0], dtype=jnp.int32)
    member = (
        (item_pos[None, :] >= start_pos[:, None]) & (item_pos[None, :] < end_pos[:, None])
    ).astype(jnp.bfloat16)
    picks = (items_here[:, None] == touch_iota[None, :]).astype(jnp.bfloat16)
    count_mat = jnp.dot(member, picks, preferred_element_type=jnp.float32)
    pooled_part = jnp.dot(count_mat, fetched, precision=HIGHEST)
    my_hot_ids = lax.dynamic_slice_in_dim(hot_ids, my_start, share_rows, 0)
    full_in = lax.all_gather(weight_in, "mp", axis=1, tiled=True)
    full_out = lax.all_gather(weight_out, "mp", axis=0, tiled=True)
    full_bias = lax.all_gather(bias_in, "mp", axis=0, tiled=True)
    pooled_mine = lax.psum_scatter(pooled_part, "mp", scatter_dimension=0, tiled=True)
    my_grads = lax.dynamic_slice_in_dim(grad_out, my_start, share_rows, 0)
    hot_rows = hot_table[my_hot_ids].reshape(share_rows, hot_cols)
    inputs = jnp.concatenate([hot_rows, pooled_mine], axis=1).astype(jnp.bfloat16)
    pre_act = jnp.dot(inputs, full_in, preferred_element_type=jnp.float32) + full_bias
    back_grad = lax.dot_general(
        my_grads, full_out, (((1,), (1,)), ((), ())), preferred_element_type=jnp.float32
    )
    hidden_grad = silu_grad(pre_act, back_grad)
    input_grad = lax.dot_general(
        hidden_grad, full_in, (((1,), (1,)), ((), ())), preferred_element_type=jnp.float32
    )
    hot_part = jax.ops.segment_sum(
        input_grad[:, :hot_cols].reshape(share_rows * fields, emb_width),
        my_hot_ids.reshape(share_rows * fields),
        num_segments=hot_table.shape[0],
    )
    bag_grad = lax.all_gather(input_grad[:, hot_cols:], "mp", axis=0, tiled=True)
    touch_grad = lax.dot_general(count_mat, bag_grad, (((0,), (0,)), ((), ())), precision=HIGHEST)
    outgoing = (
        jnp.zeros((dp_count * capacity, emb_width), jnp.float32)
        .at[bucket_pos]
        .set(touch_grad)
        .reshape(dp_count, capacity, emb_width)
    )
    arrived = exchange(outgoing, 3)
    cold_grad = jax.ops.segment_sum(
        arrived.reshape(-1, emb_width), asked_slots.reshape(-1), num_segments=slot_count
    )
    cold_updated, cold_accum_new = adagrad(cold_table, cold_accum, cold_grad)
    hot_grad = hot_allreduce(hot_part, 0)
    hot_updated, hot_accum_new = adagrad(hot_table, hot_accum, hot_grad)
    return (hot_updated, hot_accum_new, cold_updated, cold_accum_new)


def solution(mesh):
    return jax.shard_map(
        per_device,
        mesh=mesh,
        in_specs=(
            P("dp", None),
            P("dp", "mp", None),
            P("dp", "mp", None),
            P("dp", "mp", None),
            P(),
            P("dp", None),
            P(None, "mp"),
            P("mp"),
            P("mp", None),
            P(),
            P(),
            P(("dp", "mp"), None),
            P(("dp", "mp"), None),
        ),
        out_specs=(P(), P(), P(("dp", "mp"), None), P(("dp", "mp"), None)),
        check_vma=False,
    )
```

```python
import functools

import jax
import jax.numpy as jnp
from jax import lax
from jax.experimental import pallas as pl
from jax.experimental.pallas import tpu as pltpu
from jax.sharding import PartitionSpec as P

STEP_SIZE = 0.5
MESH = pl.DeviceIdType.MESH
F32, BF16, I32 = jnp.float32, jnp.bfloat16, jnp.int32
NT = (((1,), (1,)), ((), ()))


def adagrad(table_rows, accum_rows, grad_rows):
    accum_new = accum_rows + grad_rows * grad_rows
    return (table_rows - STEP_SIZE * grad_rows / jnp.sqrt(accum_new), accum_new)


def iota(shape, dim):
    return lax.broadcasted_iota(I32, shape, dim)


def mm(a, b):
    return jnp.dot(a, b, preferred_element_type=F32)


def mm_nt(a, b):
    return lax.dot_general(a, b, NT, preferred_element_type=F32)


def ones_where(mask):
    return jnp.where(mask, 1.0, 0.0).astype(BF16)


def halves(x):
    high = x.astype(BF16)
    low = (x - high.astype(F32)).astype(BF16)
    return jnp.concatenate([high, low], axis=1)


def joined(x):
    half = x.shape[1] // 2
    return x[:, :half] + x[:, half:]


def column(row):
    parts = [
        jnp.broadcast_to(row[:, k : k + 128], (128, 128)).T for k in range(0, row.shape[1], 128)
    ]
    return parts[0] if len(parts) == 1 else jnp.concatenate(parts, axis=0)


def rows_at(index, size):
    return pl.ds(pl.multiple_of(index * size, size), size)


def step_kernel(
    ids_ref, touched_ref, items_ref, counts_ref, owner_ref, grad_ref, win_ref, bias_ref, wout_ref,
    hot_ref, cold_ref, hot_grad, cold_grad,
    full_in, full_out, full_bias, req, asked, rows_out, rows_back, member, picks, bag_mat, bag_mat_t,
    gather_t, hot_in, hot_pre, back, pooled, pool_in, bag, part, part_in, acc, acc_in, sums, outgoing,
    arrived, sem_w, sem_pool, sem_bag, sem_a, sem_d, sem_x,
):
    dp, x = lax.axis_index("dp"), lax.axis_index("mp")
    core = dp % 2
    plane = dp // 2

    def near(ox):
        return (dp, (x + ox) % 4)

    barrier = pltpu.get_barrier_semaphore()
    for ox in range(1, 4):
        pl.semaphore_signal(barrier, inc=1, device_id=near(ox), device_id_type=MESH)

    @pl.loop(1, 128)
    def _(o):
        pl.semaphore_signal(barrier, inc=1, device_id=((dp + o) % 128, x), device_id_type=MESH)

    touched = column(touched_ref[0].astype(F32)).astype(I32)
    lane = iota((256, 128), 1)
    owner_row = touched >> 7
    picked = jnp.concatenate(
        [ones_where(owner_row == lane + 128 * k) for k in range(8)], axis=1
    )
    owners = owner_ref[...]
    tables = jnp.concatenate(
        [(owners >> 10).astype(F32).astype(BF16), (owners & 255).astype(F32).astype(BF16)], axis=1
    )
    found = mm(picked, tables)
    here = (touched & 127) == lane
    owner = jnp.sum(jnp.where(here, found[:, :128], 0.0), axis=1, keepdims=True)
    slot = jnp.sum(jnp.where(here, found[:, 128:], 0.0), axis=1, keepdims=True)
    lane_f = lane.astype(F32)
    hits = jnp.where(owner == lane_f, 1.0, 0.0)
    earlier = ones_where(iota((256, 256), 0) > iota((256, 256), 1))
    rank = jnp.sum(mm(earlier, hits.astype(BF16)) * hits, axis=1, keepdims=True)
    ranked = jnp.where(rank == lane_f, slot + 1.0, 0.0).astype(BF16)
    req[:, 0, :] = mm(hits.T.astype(BF16), ranked)
    bucket = owner * 4.0 + rank

    pl.semaphore_wait(barrier, 130)

    def send_all(src, dst, k):
        @pl.loop(1, 128)
        def _(o):
            to = (dp + o) % 128
            pltpu.make_async_remote_copy(
                src_ref=src.at[to], dst_ref=dst.at[dp], send_sem=sem_x.at[0, k], recv_sem=sem_x.at[1, k],
                device_id=(to, x), device_id_type=MESH,
            ).start()
        dst[dp] = src[dp]

    def wait_all(src, dst, k):
        some = dst.at[pl.ds(0, 127)]
        pltpu.make_async_copy(some, some, sem_x.at[1, k]).wait()

    def wait_sent(src, k):
        some = src.at[pl.ds(0, 127)]
        pltpu.make_async_copy(some, some, sem_x.at[0, k]).wait()

    def to_near(ox, src, dst, sems, k):
        cp = pltpu.make_async_remote_copy(
            src_ref=src, dst_ref=dst, send_sem=sems.at[0, k], recv_sem=sems.at[1, k],
            device_id=near(ox), device_id_type=MESH,
        )
        cp.start()
        return cp

    send_all(req, asked, 0)

    mine = rows_at(x, 128)
    weight_copies = []
    for ox in range(1, 4):
        weight_copies.append(to_near(ox, win_ref, full_in.at[:, mine], sem_w, ox - 1))
        weight_copies.append(to_near(ox, wout_ref, full_out.at[mine], sem_w, ox + 2))
        weight_copies.append(to_near(ox, bias_ref, full_bias.at[:, mine], sem_w, ox + 5))
    full_in[:, mine] = win_ref[...]
    full_out[mine] = wout_ref[...]
    full_bias[:, mine] = bias_ref[...]

    counts = counts_ref[0].astype(F32)
    eight = jnp.concatenate([counts[:, 128 * j : 128 * (j + 1)] for j in range(8)], axis=0)
    upto = ones_where(iota((128, 128), 0) <= iota((128, 128), 1))
    ends = mm(eight.astype(BF16), upto)
    total = jnp.zeros((1, 1), F32)
    item_pos = iota((128, 2048), 1).astype(F32)
    for j in range(8):
        end = ends[j : j + 1] + total
        total = end[:, 127:128]
        end_col = column(end)[:, :1]
        start_col = column(end - eight[j : j + 1])[:, :1]
        member[128 * j : 128 * (j + 1)] = ones_where((item_pos >= start_col) & (item_pos < end_col))
    picks[...] = ones_where(items_ref[0] == iota((256, 2048), 0))

    wait_all(req, asked, 0)

    wanted = asked[:, 0, :].astype(BF16)
    spread = mm(ones_where((iota((512, 128), 0) >> 2) == iota((512, 128), 1)), wanted)
    wanted_col = jnp.sum(
        jnp.where((iota((512, 128), 0) & 3) == iota((512, 128), 1), spread, 0.0), axis=1, keepdims=True
    )
    chosen = ones_where(wanted_col == (iota((512, 256), 1) + 1).astype(F32))
    rows_out[...] = joined(mm(chosen, halves(cold_ref[...]))).reshape(128, 4, 128)
    send_all(rows_out, rows_back, 1)

    count_mat = mm_nt(member[...], picks[...]).astype(BF16)
    spot = jnp.where(bucket == iota((256, 512), 1).astype(F32), 1.0, 0.0)
    bag_mat[...] = mm(count_mat, spot.astype(BF16)).astype(BF16)
    count_mat_t = mm_nt(picks[...], member[...]).astype(BF16)
    bag_mat_t[...] = mm(spot.T.astype(BF16), count_mat_t).astype(BF16)

    share = rows_at(x, 256)
    ids = ids_ref[:, share]
    hot_bf = hot_ref[...].astype(BF16)
    row_of = iota((1024, 256), 0)
    lane_1k = iota((256, 1024), 1).astype(F32)
    for f in range(7):
        one = ids[f : f + 1]
        gather_t[:, 256 * f : 256 * (f + 1)] = ones_where(row_of == one)
        pick_f = ones_where(column(one.astype(F32))[:, :1] == lane_1k)
        hot_in[:, 128 * f : 128 * (f + 1)] = mm(pick_f, hot_bf).astype(BF16)
    for cp in weight_copies:
        cp.wait_recv()
    hot_pre[...] = mm(hot_in[...], full_in[0:896]) + full_bias[...]
    back[...] = mm_nt(grad_ref[share], full_out[...])

    wait_all(rows_out, rows_back, 1)
    pooled[...] = joined(mm(bag_mat[...], halves(rows_back[...].reshape(512, 128))))
    pool_copies = [
        to_near(ox, pooled.at[rows_at((x + ox) % 4, 256)], pool_in.at[ox - 1], sem_pool, ox - 1)
        for ox in range(1, 4)
    ]
    pool_sum = pooled[share]
    for cp in pool_copies:
        cp.wait_recv()
    pool_sum = pool_sum + pool_in[0] + pool_in[1] + pool_in[2]

    pre = hot_pre[...] + mm(pool_sum.astype(BF16), full_in[896:1024])
    gate = jax.nn.sigmoid(pre)
    hidden = (back[...] * gate * (1.0 + pre * (1.0 - gate))).astype(BF16)
    bag[x] = mm_nt(hidden, full_in[896:1024])
    bag_copies = [to_near(ox, bag.at[x], bag.at[x], sem_bag, ox - 1) for ox in range(1, 4)]
    in_grad = jnp.concatenate(
        [halves(mm_nt(hidden, full_in[128 * f : 128 * (f + 1)])) for f in range(7)], axis=0
    )

    a_copies = []
    for oc, ox in ((1, 2), (0, 2), (1, 1), (1, 3), (0, 1), (0, 3), (1, 0), (0, 0)):
        there = rows_at(((core + oc) % 2) * 4 + (x + ox) % 4, 128)
        part[there] = joined(mm(gather_t[there], in_grad))
        k = oc * 4 + ox
        if k:
            cp = pltpu.make_async_remote_copy(
                src_ref=part.at[there], dst_ref=part_in.at[k - 1], send_sem=sem_a.at[0, k - 1],
                recv_sem=sem_a.at[1, k - 1], device_id=(plane * 2 + (core + oc) % 2, (x + ox) % 4),
                device_id_type=MESH,
            )
            cp.start()
            a_copies.append(cp)
    for cp in a_copies:
        cp.wait_recv()
    block = part[rows_at(core * 4 + x, 128)]
    for k in range(7):
        block = block + part_in[k]
    acc[...] = block.reshape(64, 2, 128)

    @pl.loop(1, 64)
    def _(o):
        to = (plane + o) % 64
        pltpu.make_async_remote_copy(
            src_ref=acc.at[to], dst_ref=acc_in.at[plane], send_sem=sem_x.at[0, 2], recv_sem=sem_x.at[1, 2],
            device_id=(to * 2 + core, x), device_id_type=MESH,
        ).start()

    acc_in[plane] = acc[plane]

    for cp in bag_copies:
        cp.wait_recv()
    bag_all = halves(bag[...].reshape(1024, 128))
    outgoing[...] = joined(mm(bag_mat_t[...], bag_all)).reshape(128, 4, 128)

    pltpu.make_async_copy(acc_in.at[pl.ds(0, 63)], acc_in.at[pl.ds(0, 63)], sem_x.at[1, 2]).wait()
    sums[plane] = jnp.sum(acc_in[...], axis=0)

    @pl.loop(1, 64)
    def _(o):
        to = (plane + o) % 64
        pltpu.make_async_remote_copy(
            src_ref=sums.at[plane], dst_ref=sums.at[plane], send_sem=sem_x.at[0, 3], recv_sem=sem_x.at[1, 3],
            device_id=(to * 2 + core, x), device_id_type=MESH,
        ).start()

    send_all(outgoing, arrived, 4)
    wanted_rows = jnp.broadcast_to(wanted_col, (512, 128)).T[0:1]
    chosen_t = ones_where(wanted_rows == (iota((256, 512), 0) + 1).astype(F32))
    pltpu.make_async_copy(sums.at[pl.ds(0, 63)], sums.at[pl.ds(0, 63)], sem_x.at[1, 3]).wait()

    own = rows_at(core * 4 + x, 128)
    hot_grad[own] = sums[...].reshape(128, 128)
    d_copies = []

    def spread_block(rows, to, k):
        cp = pltpu.make_async_remote_copy(
            src_ref=hot_grad.at[rows], dst_ref=hot_grad.at[rows], send_sem=sem_d.at[0, k],
            recv_sem=sem_d.at[1, k], device_id=to, device_id_type=MESH,
        )
        cp.start()
        return cp

    sibling = (plane * 2 + 1 - core, x)
    d_copies = [spread_block(own, near(ox), ox - 1) for ox in range(1, 4)]
    forwards = [spread_block(own, sibling, 3)]
    for ox in (1, 3, 2):
        d_copies[ox - 1].wait_recv()
        forwards.append(spread_block(rows_at(core * 4 + (x + 4 - ox) % 4, 128), sibling, 3 + ox))

    wait_all(outgoing, arrived, 4)
    cold_grad[...] = joined(mm(chosen_t, halves(arrived[...].reshape(512, 128))))
    for cp in forwards:
        cp.wait_recv()

    for cp in weight_copies + pool_copies + bag_copies + a_copies + d_copies + forwards:
        cp.wait_send()
    wait_sent(req, 0)
    wait_sent(rows_out, 1)
    wait_sent(outgoing, 4)
    pltpu.make_async_copy(acc.at[pl.ds(0, 63)], acc.at[pl.ds(0, 63)], sem_x.at[0, 2]).wait()
    pltpu.make_async_copy(sums.at[pl.ds(0, 63)], sums.at[pl.ds(0, 63)], sem_x.at[0, 3]).wait()


def per_device(
    hot_ids, touched, cold_items, bag_counts, owner_map, grad_out, weight_in, bias_in, weight_out,
    hot_table, hot_accum, cold_table, cold_accum,
):
    vmem = pl.BlockSpec(memory_space=pltpu.VMEM)
    v = pltpu.VMEM
    dma = pltpu.SemaphoreType.DMA
    hot_grad, cold_grad = pl.pallas_call(
        step_kernel,
        out_shape=(jax.ShapeDtypeStruct((1024, 128), F32), jax.ShapeDtypeStruct((256, 128), F32)),
        in_specs=[vmem] * 11,
        out_specs=(vmem, vmem),
        scratch_shapes=[
            v((1024, 512), BF16), v((512, 256), BF16), v((1, 512), F32),
            v((128, 1, 128), F32), v((128, 1, 128), F32),
            v((128, 4, 128), F32), v((128, 4, 128), F32),
            v((1024, 2048), BF16), v((256, 2048), BF16), v((1024, 512), BF16), v((512, 1024), BF16),
            v((1024, 1792), BF16), v((256, 896), BF16), v((256, 512), F32), v((256, 512), F32),
            v((1024, 128), F32), v((3, 256, 128), F32), v((4, 256, 128), F32),
            v((1024, 128), F32), v((7, 128, 128), F32), v((64, 2, 128), F32), v((64, 2, 128), F32),
            v((64, 2, 128), F32),
            v((128, 4, 128), F32), v((128, 4, 128), F32),
            dma((2, 9)), dma((2, 3)), dma((2, 3)), dma((2, 7)), dma((2, 7)), dma((2, 5)),
        ],
        compiler_params=pltpu.CompilerParams(
            collective_id=0, has_side_effects=True, vmem_limit_bytes=56 << 20
        ),
        name="step",
    )(
        hot_ids.T, touched, cold_items, bag_counts, owner_map.reshape(1024, 128), grad_out, weight_in,
        bias_in.reshape(1, 128), weight_out, hot_table, cold_table,
    )
    cold_updated, cold_accum_new = adagrad(cold_table, cold_accum, cold_grad)
    hot_updated, hot_accum_new = adagrad(hot_table, hot_accum, hot_grad)
    return (hot_updated, hot_accum_new, cold_updated, cold_accum_new)


def solution(mesh):
    return jax.shard_map(
        per_device,
        mesh=mesh,
        in_specs=(
            P("dp", None),
            P("dp", "mp", None),
            P("dp", "mp", None),
            P("dp", "mp", None),
            P(),
            P("dp", None),
            P(None, "mp"),
            P("mp"),
            P("mp", None),
            P(),
            P(),
            P(("dp", "mp"), None),
            P(("dp", "mp"), None),
        ),
        out_specs=(P(), P(), P(("dp", "mp"), None), P(("dp", "mp"), None)),
        check_vma=False,
    )
```

```python
import functools

import jax
import jax.numpy as jnp
from jax import lax
from jax.experimental import pallas as pl
from jax.experimental.pallas import tpu as pltpu
from jax.sharding import PartitionSpec as P

STEP_SIZE = 0.5
MESH = pl.DeviceIdType.MESH
F32, BF16, I32 = jnp.float32, jnp.bfloat16, jnp.int32
NT = (((1,), (1,)), ((), ()))


def adagrad_kernel(hot_grad, cold_grad, hot, hot_acc, cold, cold_acc, hot_new, hot_acc_new, cold_new, cold_acc_new):
    for grad, table, accum, table_new, accum_new in (
        (hot_grad, hot, hot_acc, hot_new, hot_acc_new),
        (cold_grad, cold, cold_acc, cold_new, cold_acc_new),
    ):
        g = grad[...]
        a = accum[...] + g * g
        accum_new[...] = a
        table_new[...] = table[...] - STEP_SIZE * g * lax.rsqrt(a)


def iota(shape, dim):
    return lax.broadcasted_iota(I32, shape, dim)


def mm(a, b):
    return jnp.dot(a, b, preferred_element_type=F32)


def mm_nt(a, b):
    return lax.dot_general(a, b, NT, preferred_element_type=F32)


def ones_where(mask):
    return jnp.where(mask, 1.0, 0.0).astype(BF16)


def halves(x):
    high = x.astype(BF16)
    low = (x - high.astype(F32)).astype(BF16)
    return jnp.concatenate([high, low], axis=1)


def joined(x):
    half = x.shape[1] // 2
    return x[:, :half] + x[:, half:]


def column(row):
    parts = [
        jnp.broadcast_to(row[:, k : k + 128], (128, 128)).T for k in range(0, row.shape[1], 128)
    ]
    return parts[0] if len(parts) == 1 else jnp.concatenate(parts, axis=0)


def rows_at(index, size):
    return pl.ds(pl.multiple_of(index * size, size), size)


def step_kernel(
    ids_ref, touched_ref, items_ref, counts_ref, owner_ref, grad_ref, win_ref, bias_ref, wout_ref,
    hot_ref, cold_ref, hot_grad, cold_grad,
    full_in, full_out, full_bias, req, asked, rows_out, rows_back, member, picks, bag_mat, bag_mat_t,
    gather_t, hot_in, hot_pre, back, pooled, pool_in, bag, part, part_in, acc, acc_in, sums, outgoing,
    arrived, hot_own, cold_own, grad_own, sem_l, sem_w, sem_pool, sem_bag, sem_a, sem_d, sem_x,
):
    dp, x = lax.axis_index("dp"), lax.axis_index("mp")
    core = dp % 2
    plane = dp // 2

    def near(ox):
        return (dp, (x + ox) % 4)

    barrier = pltpu.get_barrier_semaphore()
    for ox in range(1, 4):
        pl.semaphore_signal(barrier, inc=1, device_id=near(ox), device_id_type=MESH)

    for o in range(1, 128):
        pl.semaphore_signal(barrier, inc=1, device_id=((dp + o) % 128, x), device_id_type=MESH)

    share = rows_at(x, 256)
    mine = rows_at(x, 128)
    local = [
        pltpu.make_async_copy(src, dst, sem_l.at[k])
        for k, (src, dst) in enumerate((
            (cold_ref, cold_own), (win_ref, full_in.at[:, mine]), (wout_ref, full_out.at[mine]),
            (bias_ref, full_bias.at[:, mine]), (hot_ref, hot_own), (grad_ref.at[share], grad_own),
        ))
    ]
    for cp in local:
        cp.start()

    touched = column(touched_ref[0].astype(F32)).astype(I32)
    lane = iota((256, 128), 1)
    owner_row = touched >> 7
    picked = jnp.concatenate(
        [ones_where(owner_row == lane + 128 * k) for k in range(8)], axis=1
    )
    owners = owner_ref[...]
    tables = jnp.concatenate(
        [(owners >> 10).astype(F32).astype(BF16), (owners & 255).astype(F32).astype(BF16)], axis=1
    )
    found = mm(picked, tables)
    here = (touched & 127) == lane
    owner = jnp.sum(jnp.where(here, found[:, :128], 0.0), axis=1, keepdims=True)
    slot = jnp.sum(jnp.where(here, found[:, 128:], 0.0), axis=1, keepdims=True)
    lane_f = lane.astype(F32)
    hits = jnp.where(owner == lane_f, 1.0, 0.0)
    earlier = ones_where(iota((256, 256), 0) > iota((256, 256), 1))
    rank = jnp.sum(mm(earlier, hits.astype(BF16)) * hits, axis=1, keepdims=True)
    ranked = jnp.where(rank == lane_f, slot + 1.0, 0.0).astype(BF16)
    req[:, 0, :] = mm(hits.T.astype(BF16), ranked)
    bucket = owner * 4.0 + rank

    pl.semaphore_wait(barrier, 130)

    def send_all(src, dst, k):
        @pl.loop(1, 128)
        def _(o):
            to = (dp + o) % 128
            pltpu.make_async_remote_copy(
                src_ref=src.at[to], dst_ref=dst.at[dp], send_sem=sem_x.at[0, k], recv_sem=sem_x.at[1, k],
                device_id=(to, x), device_id_type=MESH,
            ).start()
        dst[dp] = src[dp]

    def wait_all(src, dst, k):
        some = dst.at[pl.ds(0, 127)]
        pltpu.make_async_copy(some, some, sem_x.at[1, k]).wait()

    def wait_sent(src, k):
        some = src.at[pl.ds(0, 127)]
        pltpu.make_async_copy(some, some, sem_x.at[0, k]).wait()

    def to_near(ox, src, dst, sems, k):
        cp = pltpu.make_async_remote_copy(
            src_ref=src, dst_ref=dst, send_sem=sems.at[0, k], recv_sem=sems.at[1, k],
            device_id=near(ox), device_id_type=MESH,
        )
        cp.start()
        return cp

    send_all(req, asked, 0)

    weight_copies = []
    for ox in range(1, 4):
        weight_copies.append(to_near(ox, win_ref, full_in.at[:, mine], sem_w, ox - 1))
        weight_copies.append(to_near(ox, wout_ref, full_out.at[mine], sem_w, ox + 2))
        weight_copies.append(to_near(ox, bias_ref, full_bias.at[:, mine], sem_w, ox + 5))

    counts = counts_ref[0].astype(F32)
    eight = jnp.concatenate([counts[:, 128 * j : 128 * (j + 1)] for j in range(8)], axis=0)
    upto = ones_where(iota((128, 128), 0) <= iota((128, 128), 1))
    ends = mm(eight.astype(BF16), upto)
    total = jnp.zeros((1, 1), F32)
    item_pos = iota((128, 2048), 1).astype(F32)
    for j in range(8):
        end = ends[j : j + 1] + total
        total = end[:, 127:128]
        end_col = column(end)[:, :1]
        start_col = column(end - eight[j : j + 1])[:, :1]
        member[128 * j : 128 * (j + 1)] = ones_where((item_pos >= start_col) & (item_pos < end_col))
    picks[...] = ones_where(items_ref[0] == iota((256, 2048), 0))
    local[0].wait()
    cold_halves = halves(cold_own[...])

    wait_all(req, asked, 0)

    wanted = asked[:, 0, :].astype(BF16)
    spread = mm(ones_where((iota((512, 128), 0) >> 2) == iota((512, 128), 1)), wanted)
    wanted_col = jnp.sum(
        jnp.where((iota((512, 128), 0) & 3) == iota((512, 128), 1), spread, 0.0), axis=1, keepdims=True
    )
    chosen = ones_where(wanted_col == (iota((512, 256), 1) + 1).astype(F32))
    rows_out[...] = joined(mm(chosen, cold_halves)).reshape(128, 4, 128)
    send_all(rows_out, rows_back, 1)

    count_mat = mm_nt(member[...], picks[...]).astype(BF16)
    spot = jnp.where(bucket == iota((256, 512), 1).astype(F32), 1.0, 0.0)
    bag_mat[...] = mm(count_mat, spot.astype(BF16)).astype(BF16)
    count_mat_t = mm_nt(picks[...], member[...]).astype(BF16)
    bag_mat_t[...] = mm(spot.T.astype(BF16), count_mat_t).astype(BF16)

    for cp in local[1:]:
        cp.wait()
    ids = ids_ref[:, share]
    hot_bf = hot_own[...].astype(BF16)
    row_of = iota((1024, 256), 0)
    lane_1k = iota((256, 1024), 1).astype(F32)
    for f in range(7):
        one = ids[f : f + 1]
        gather_t[:, 256 * f : 256 * (f + 1)] = ones_where(row_of == one)
        pick_f = ones_where(column(one.astype(F32))[:, :1] == lane_1k)
        hot_in[:, 128 * f : 128 * (f + 1)] = mm(pick_f, hot_bf).astype(BF16)
    for cp in weight_copies:
        cp.wait_recv()
    hot_pre[...] = mm(hot_in[...], full_in[0:896]) + full_bias[...]
    back[...] = mm_nt(grad_own[...], full_out[...])

    wait_all(rows_out, rows_back, 1)
    rows = halves(rows_back[...].reshape(512, 128))
    pool_copies = []
    for ox in (2, 1, 3):
        there = rows_at((x + ox) % 4, 256)
        pooled[there] = joined(mm(bag_mat[there], rows)).astype(BF16)
        pool_copies.append(to_near(ox, pooled.at[there], pool_in.at[ox - 1], sem_pool, ox - 1))
    pool_sum = joined(mm(bag_mat[share], rows))
    for cp in pool_copies:
        cp.wait_recv()
    for k in range(3):
        pool_sum = pool_sum + pool_in[k].astype(F32)

    pre = hot_pre[...] + mm(pool_sum.astype(BF16), full_in[896:1024])
    gate = jax.nn.sigmoid(pre)
    hidden = (back[...] * gate * (1.0 + pre * (1.0 - gate))).astype(BF16)
    bag[x] = mm_nt(hidden, full_in[896:1024])
    in_grad = jnp.concatenate(
        [halves(mm_nt(hidden, full_in[128 * f : 128 * (f + 1)])) for f in range(7)], axis=0
    )

    a_copies = []
    for oc, ox in ((1, 2), (0, 2), (1, 1), (1, 3), (0, 1), (0, 3), (1, 0), (0, 0)):
        there = rows_at(((core + oc) % 2) * 4 + (x + ox) % 4, 128)
        part[there] = joined(mm(gather_t[there], in_grad))
        k = oc * 4 + ox
        if k:
            cp = pltpu.make_async_remote_copy(
                src_ref=part.at[there], dst_ref=part_in.at[k - 1], send_sem=sem_a.at[0, k - 1],
                recv_sem=sem_a.at[1, k - 1], device_id=(plane * 2 + (core + oc) % 2, (x + ox) % 4),
                device_id_type=MESH,
            )
            cp.start()
            a_copies.append(cp)
    bag_copies = [to_near(ox, bag.at[x], bag.at[x], sem_bag, ox - 1) for ox in (2, 1, 3)]
    for cp in a_copies:
        cp.wait_recv()
    block = part[rows_at(core * 4 + x, 128)]
    for k in range(7):
        block = block + part_in[k]
    acc[...] = block.reshape(64, 2, 128)

    @pl.loop(1, 64)
    def _(o):
        to = (plane + o) % 64
        pltpu.make_async_remote_copy(
            src_ref=acc.at[to], dst_ref=acc_in.at[plane], send_sem=sem_x.at[0, 2], recv_sem=sem_x.at[1, 2],
            device_id=(to * 2 + core, x), device_id_type=MESH,
        ).start()

    acc_in[plane] = acc[plane]

    pltpu.make_async_copy(acc_in.at[pl.ds(0, 63)], acc_in.at[pl.ds(0, 63)], sem_x.at[1, 2]).wait()
    sums[plane] = jnp.sum(acc_in[...], axis=0)

    @pl.loop(1, 64)
    def _(o):
        to = (plane + o) % 64
        pltpu.make_async_remote_copy(
            src_ref=sums.at[plane], dst_ref=sums.at[plane], send_sem=sem_x.at[0, 3], recv_sem=sem_x.at[1, 3],
            device_id=(to * 2 + core, x), device_id_type=MESH,
        ).start()

    for cp in bag_copies:
        cp.wait_recv()
    bag_all = halves(bag[...].reshape(1024, 128))
    outgoing[...] = joined(mm(bag_mat_t[...], bag_all)).reshape(128, 4, 128)

    send_all(outgoing, arrived, 4)
    wanted_rows = jnp.broadcast_to(wanted_col, (512, 128)).T[0:1]
    chosen_t = ones_where(wanted_rows == (iota((256, 512), 0) + 1).astype(F32))
    pltpu.make_async_copy(sums.at[pl.ds(0, 63)], sums.at[pl.ds(0, 63)], sem_x.at[1, 3]).wait()

    own = rows_at(core * 4 + x, 128)
    hot_grad[own] = sums[...].reshape(128, 128)

    def spread_block(rows, to, k):
        cp = pltpu.make_async_remote_copy(
            src_ref=hot_grad.at[rows], dst_ref=hot_grad.at[rows], send_sem=sem_d.at[0, k],
            recv_sem=sem_d.at[1, k], device_id=to, device_id_type=MESH,
        )
        cp.start()
        return cp

    sibling = (plane * 2 + 1 - core, x)
    d_copies = [spread_block(own, near(ox), ox - 1) for ox in (1, 2, 3)]
    forwards = [spread_block(own, sibling, 3)]
    for ox in (1, 3, 2):
        d_copies[ox - 1].wait_recv()
        forwards.append(spread_block(rows_at(core * 4 + (x + 4 - ox) % 4, 128), sibling, 3 + ox))

    wait_all(outgoing, arrived, 4)
    cold_grad[...] = joined(mm(chosen_t, halves(arrived[...].reshape(512, 128))))
    for cp in forwards:
        cp.wait_recv()

    for cp in weight_copies + pool_copies + bag_copies + a_copies + d_copies + forwards:
        cp.wait_send()
    wait_sent(req, 0)
    wait_sent(rows_out, 1)
    wait_sent(outgoing, 4)
    pltpu.make_async_copy(acc.at[pl.ds(0, 63)], acc.at[pl.ds(0, 63)], sem_x.at[0, 2]).wait()
    pltpu.make_async_copy(sums.at[pl.ds(0, 63)], sums.at[pl.ds(0, 63)], sem_x.at[0, 3]).wait()


def per_device(
    hot_ids, touched, cold_items, bag_counts, owner_map, grad_out, weight_in, bias_in, weight_out,
    hot_table, hot_accum, cold_table, cold_accum,
):
    vmem = pl.BlockSpec(memory_space=pltpu.VMEM)
    v = pltpu.VMEM
    dma = pltpu.SemaphoreType.DMA
    hot_grad, cold_grad = pl.pallas_call(
        step_kernel,
        out_shape=(v((1024, 128), F32), v((256, 128), F32)),
        in_specs=[vmem] * 5 + [pl.BlockSpec(memory_space=pl.ANY)] * 6,
        out_specs=(vmem, vmem),
        scratch_shapes=[
            v((1024, 512), BF16), v((512, 256), BF16), v((1, 512), F32),
            v((128, 1, 128), F32), v((128, 1, 128), F32),
            v((128, 4, 128), F32), v((128, 4, 128), F32),
            v((1024, 2048), BF16), v((256, 2048), BF16), v((1024, 512), BF16), v((512, 1024), BF16),
            v((1024, 1792), BF16), v((256, 896), BF16), v((256, 512), F32), v((256, 512), F32),
            v((1024, 128), BF16), v((3, 256, 128), BF16), v((4, 256, 128), F32),
            v((1024, 128), F32), v((7, 128, 128), F32), v((64, 2, 128), F32), v((64, 2, 128), F32),
            v((64, 2, 128), F32),
            v((128, 4, 128), F32), v((128, 4, 128), F32),
            v((1024, 128), F32), v((256, 128), F32), v((256, 256), BF16), dma((6,)),
            dma((2, 9)), dma((2, 3)), dma((2, 3)), dma((2, 7)), dma((2, 7)), dma((2, 5)),
        ],
        compiler_params=pltpu.CompilerParams(
            collective_id=0, has_side_effects=True, vmem_limit_bytes=56 << 20
        ),
        name="step",
    )(
        hot_ids.T, touched, cold_items, bag_counts, owner_map.reshape(1024, 128), grad_out, weight_in,
        bias_in.reshape(1, 128), weight_out, hot_table, cold_table,
    )
    return pl.pallas_call(
        adagrad_kernel,
        out_shape=tuple(jax.ShapeDtypeStruct(r.shape, F32) for r in (hot_table, hot_accum, cold_table, cold_accum)),
        in_specs=[vmem] * 6,
        out_specs=(vmem,) * 4,
        compiler_params=pltpu.CompilerParams(vmem_limit_bytes=16 << 20),
        name="adagrad",
    )(hot_grad, cold_grad, hot_table, hot_accum, cold_table, cold_accum)


def solution(mesh):
    return jax.shard_map(
        per_device,
        mesh=mesh,
        in_specs=(
            P("dp", None),
            P("dp", "mp", None),
            P("dp", "mp", None),
            P("dp", "mp", None),
            P(),
            P("dp", None),
            P(None, "mp"),
            P("mp"),
            P("mp", None),
            P(),
            P(),
            P(("dp", "mp"), None),
            P(("dp", "mp"), None),
        ),
        out_specs=(P(), P(), P(("dp", "mp"), None), P(("dp", "mp"), None)),
        check_vma=False,
    )
```

```python
import functools

import jax
import jax.numpy as jnp
from jax import lax
from jax.experimental import pallas as pl
from jax.experimental.pallas import tpu as pltpu
from jax.sharding import PartitionSpec as P

STEP_SIZE = 0.5
MESH = pl.DeviceIdType.MESH
F32, BF16, I32 = jnp.float32, jnp.bfloat16, jnp.int32
NT = (((1,), (1,)), ((), ()))


def adagrad_kernel(hot_grad, cold_grad, hot, hot_acc, cold, cold_acc, hot_new, hot_acc_new, cold_new, cold_acc_new):
    for grad, table, accum, table_new, accum_new in (
        (hot_grad, hot, hot_acc, hot_new, hot_acc_new),
        (cold_grad, cold, cold_acc, cold_new, cold_acc_new),
    ):
        g = grad[...]
        a = accum[...] + g * g
        accum_new[...] = a
        table_new[...] = table[...] - STEP_SIZE * g * lax.rsqrt(a)


def iota(shape, dim):
    return lax.broadcasted_iota(I32, shape, dim)


def mm(a, b):
    return jnp.dot(a, b, preferred_element_type=F32)


def mm_nt(a, b):
    return lax.dot_general(a, b, NT, preferred_element_type=F32)


def ones_where(mask):
    return jnp.where(mask, 1.0, 0.0).astype(BF16)


def halves(x):
    high = x.astype(BF16)
    low = (x - high.astype(F32)).astype(BF16)
    return jnp.concatenate([high, low], axis=1)


def joined(x):
    half = x.shape[1] // 2
    return x[:, :half] + x[:, half:]


def column(row):
    parts = [
        jnp.broadcast_to(row[:, k : k + 128], (128, 128)).T for k in range(0, row.shape[1], 128)
    ]
    return parts[0] if len(parts) == 1 else jnp.concatenate(parts, axis=0)


def rows_at(index, size):
    return pl.ds(pl.multiple_of(index * size, size), size)


def step_kernel(
    ids_ref, touched_ref, items_ref, counts_ref, owner_ref, grad_ref, win_ref, bias_ref, wout_ref,
    hot_ref, cold_ref, hot_grad, cold_grad,
    full_in, full_out, full_bias, req, asked, rows_out, rows_back, member, picks, bag_mat, bag_mat_t,
    gather_t, hot_in, hot_pre, back, pooled, pool_in, bag, part, part_in, acc, acc_in, sums, outgoing,
    arrived, hot_own, cold_own, grad_own, owner_own, sem_l, sem_f, sem_w, sem_pool, sem_bag, sem_a, sem_d, sem_x,
):
    dp, x = lax.axis_index("dp"), lax.axis_index("mp")
    core = dp % 2
    plane = dp // 2
    sibling = (plane * 2 + 1 - core, x)

    def near(ox):
        return (dp, (x + ox) % 4)

    share = rows_at(x, 256)
    mine = rows_at(x, 128)
    local = [
        pltpu.make_async_copy(src, dst, sem_l.at[k])
        for k, (src, dst) in enumerate((
            (owner_ref, owner_own),
            (cold_ref, cold_own), (win_ref, full_in.at[:, mine]), (wout_ref, full_out.at[mine]),
            (bias_ref, full_bias.at[:, mine]), (hot_ref, hot_own), (grad_ref.at[share], grad_own),
        ))
    ]
    for cp in local:
        cp.start()

    barrier = pltpu.get_barrier_semaphore()
    for ox in range(1, 4):
        pl.semaphore_signal(barrier, inc=1, device_id=near(ox), device_id_type=MESH)

    for o in range(1, 128):
        pl.semaphore_signal(barrier, inc=1, device_id=((dp + o) % 128, x), device_id_type=MESH)

    touched = column(touched_ref[0].astype(F32)).astype(I32)
    lane = iota((256, 128), 1)
    owner_row = touched >> 7
    picked = jnp.concatenate(
        [ones_where(owner_row == lane + 128 * k) for k in range(8)], axis=1
    )
    local[0].wait()
    owners = owner_own[...]
    tables = jnp.concatenate(
        [(owners >> 10).astype(F32).astype(BF16), (owners & 255).astype(F32).astype(BF16)], axis=1
    )
    found = mm(picked, tables)
    here = (touched & 127) == lane
    owner = jnp.sum(jnp.where(here, found[:, :128], 0.0), axis=1, keepdims=True)
    slot = jnp.sum(jnp.where(here, found[:, 128:], 0.0), axis=1, keepdims=True)
    lane_f = lane.astype(F32)
    hits = jnp.where(owner == lane_f, 1.0, 0.0)
    earlier = ones_where(iota((256, 256), 0) > iota((256, 256), 1))
    rank = jnp.sum(mm(earlier, hits.astype(BF16)) * hits, axis=1, keepdims=True)
    ranked = jnp.where(rank == lane_f, slot + 1.0, 0.0).astype(BF16)
    req[:, 0, :] = mm(hits.T.astype(BF16), ranked)
    bucket = owner * 4.0 + rank

    pl.semaphore_wait(barrier, 130)

    def send_all(src, dst, k):
        @pl.loop(1, 128)
        def _(o):
            to = (dp + o) % 128
            pltpu.make_async_remote_copy(
                src_ref=src.at[to], dst_ref=dst.at[dp], send_sem=sem_x.at[0, k], recv_sem=sem_x.at[1, k],
                device_id=(to, x), device_id_type=MESH,
            ).start()
        dst[dp] = src[dp]

    def wait_all(src, dst, k):
        some = dst.at[pl.ds(0, 127)]
        pltpu.make_async_copy(some, some, sem_x.at[1, k]).wait()

    def wait_sent(src, k):
        some = src.at[pl.ds(0, 127)]
        pltpu.make_async_copy(some, some, sem_x.at[0, k]).wait()

    def to_near(ox, src, dst, sems, k):
        cp = pltpu.make_async_remote_copy(
            src_ref=src, dst_ref=dst, send_sem=sems.at[0, k], recv_sem=sems.at[1, k],
            device_id=near(ox), device_id_type=MESH,
        )
        cp.start()
        return cp

    half_in = rows_at(core, 512)
    half_out = rows_at(core, 64)

    def out_rows(index):
        return pl.ds(pl.multiple_of(index * 128 + core * 64, 64), 64)

    weight_copies = {}
    for ox in (2, 1, 3):
        weight_copies[ox] = (
            to_near(ox, win_ref.at[half_in], full_in.at[half_in, mine], sem_w, ox - 1),
            to_near(ox, wout_ref.at[half_out], full_out.at[out_rows(x)], sem_w, ox + 2),
            to_near(ox, bias_ref, full_bias.at[:, mine], sem_w, ox + 5),
        )
    send_all(req, asked, 0)

    counts = counts_ref[0].astype(F32)
    eight = jnp.concatenate([counts[:, 128 * j : 128 * (j + 1)] for j in range(8)], axis=0)
    upto = ones_where(iota((128, 128), 0) <= iota((128, 128), 1))
    ends = mm(eight.astype(BF16), upto)
    total = jnp.zeros((1, 1), F32)
    item_pos = iota((128, 2048), 1).astype(F32)
    for j in range(8):
        end = ends[j : j + 1] + total
        total = end[:, 127:128]
        end_col = column(end)[:, :1]
        start_col = column(end - eight[j : j + 1])[:, :1]
        member[128 * j : 128 * (j + 1)] = ones_where((item_pos >= start_col) & (item_pos < end_col))
    picks[...] = ones_where(items_ref[0] == iota((256, 2048), 0))
    local[1].wait()
    cold_halves = halves(cold_own[...])

    wait_all(req, asked, 0)

    wanted = asked[:, 0, :].astype(BF16)
    spread = mm(ones_where((iota((512, 128), 0) >> 2) == iota((512, 128), 1)), wanted)
    wanted_col = jnp.sum(
        jnp.where((iota((512, 128), 0) & 3) == iota((512, 128), 1), spread, 0.0), axis=1, keepdims=True
    )
    chosen = ones_where(wanted_col == (iota((512, 256), 1) + 1).astype(F32))
    rows_out[...] = joined(mm(chosen, cold_halves)).reshape(128, 4, 128)
    send_all(rows_out, rows_back, 1)

    def to_sibling(ref, k):
        cp = pltpu.make_async_remote_copy(
            src_ref=ref, dst_ref=ref, send_sem=sem_f.at[0, k], recv_sem=sem_f.at[1, k],
            device_id=sibling, device_id_type=MESH,
        )
        cp.start()
        return cp

    weight_hands = []
    for ox in (1, 3, 2):
        for cp in weight_copies[ox]:
            cp.wait_recv()
        origin = (x + 4 - ox) % 4
        weight_hands.append(to_sibling(full_in.at[half_in, rows_at(origin, 128)], ox - 1))
        weight_hands.append(to_sibling(full_out.at[out_rows(origin)], ox + 2))

    count_mat = mm_nt(member[...], picks[...]).astype(BF16)
    spot = jnp.where(bucket == iota((256, 512), 1).astype(F32), 1.0, 0.0)
    bag_mat[...] = mm(count_mat, spot.astype(BF16)).astype(BF16)
    count_mat_t = mm_nt(picks[...], member[...]).astype(BF16)
    bag_mat_t[...] = mm(spot.T.astype(BF16), count_mat_t).astype(BF16)

    for cp in local[2:]:
        cp.wait()
    ids = ids_ref[:, share]
    hot_bf = hot_own[...].astype(BF16)
    row_of = iota((1024, 256), 0)
    lane_1k = iota((256, 1024), 1).astype(F32)
    for f in range(7):
        one = ids[f : f + 1]
        gather_t[:, 256 * f : 256 * (f + 1)] = ones_where(row_of == one)
        pick_f = ones_where(column(one.astype(F32))[:, :1] == lane_1k)
        hot_in[:, 128 * f : 128 * (f + 1)] = mm(pick_f, hot_bf).astype(BF16)
    for cp in weight_hands:
        cp.wait_recv()
    hot_pre[...] = mm(hot_in[...], full_in[0:896]) + full_bias[...]
    back[...] = mm_nt(grad_own[...], full_out[...])

    wait_all(rows_out, rows_back, 1)
    rows = halves(rows_back[...].reshape(512, 128))
    pool_copies = []
    for ox in (2, 1, 3):
        there = rows_at((x + ox) % 4, 256)
        pooled[there] = joined(mm(bag_mat[there], rows)).astype(BF16)
        pool_copies.append(to_near(ox, pooled.at[there], pool_in.at[ox - 1], sem_pool, ox - 1))
    pool_sum = joined(mm(bag_mat[share], rows))
    for cp in pool_copies:
        cp.wait_recv()
    for k in range(3):
        pool_sum = pool_sum + pool_in[k].astype(F32)

    pre = hot_pre[...] + mm(pool_sum.astype(BF16), full_in[896:1024])
    gate = jax.nn.sigmoid(pre)
    hidden = (back[...] * gate * (1.0 + pre * (1.0 - gate))).astype(BF16)
    bag[x] = mm_nt(hidden, full_in[896:1024])
    in_grad = jnp.concatenate(
        [halves(mm_nt(hidden, full_in[128 * f : 128 * (f + 1)])) for f in range(7)], axis=0
    )

    a_copies = []
    for oc in (1, 0):
        side = (core + oc) % 2
        half = rows_at(side, 512)
        part[half] = joined(mm(gather_t[half], in_grad))
        for ox in (2, 1, 3, 0):
            k = oc * 4 + ox
            if k:
                cp = pltpu.make_async_remote_copy(
                    src_ref=part.at[rows_at(side * 4 + (x + ox) % 4, 128)], dst_ref=part_in.at[k - 1],
                    send_sem=sem_a.at[0, k - 1], recv_sem=sem_a.at[1, k - 1],
                    device_id=(plane * 2 + side, (x + ox) % 4), device_id_type=MESH,
                )
                cp.start()
                a_copies.append(cp)
    bag_copies = [to_near(ox, bag.at[x], bag.at[x], sem_bag, ox - 1) for ox in (2, 1, 3)]
    for cp in a_copies:
        cp.wait_recv()
    block = part[rows_at(core * 4 + x, 128)]
    for k in range(7):
        block = block + part_in[k]
    acc[...] = block.reshape(64, 2, 128)

    @pl.loop(1, 64)
    def _(o):
        to = (plane + o) % 64
        pltpu.make_async_remote_copy(
            src_ref=acc.at[to], dst_ref=acc_in.at[plane], send_sem=sem_x.at[0, 2], recv_sem=sem_x.at[1, 2],
            device_id=(to * 2 + core, x), device_id_type=MESH,
        ).start()

    acc_in[plane] = acc[plane]

    pltpu.make_async_copy(acc_in.at[pl.ds(0, 63)], acc_in.at[pl.ds(0, 63)], sem_x.at[1, 2]).wait()
    sums[plane] = jnp.sum(acc_in[...], axis=0)

    @pl.loop(1, 64)
    def _(o):
        to = (plane + o) % 64
        pltpu.make_async_remote_copy(
            src_ref=sums.at[plane], dst_ref=sums.at[plane], send_sem=sem_x.at[0, 3], recv_sem=sem_x.at[1, 3],
            device_id=(to * 2 + core, x), device_id_type=MESH,
        ).start()

    for cp in bag_copies:
        cp.wait_recv()
    bag_all = halves(bag[...].reshape(1024, 128))
    outgoing[...] = joined(mm(bag_mat_t[...], bag_all)).reshape(128, 4, 128)

    send_all(outgoing, arrived, 4)
    wanted_rows = jnp.broadcast_to(wanted_col, (512, 128)).T[0:1]
    chosen_t = ones_where(wanted_rows == (iota((256, 512), 0) + 1).astype(F32))
    pltpu.make_async_copy(sums.at[pl.ds(0, 63)], sums.at[pl.ds(0, 63)], sem_x.at[1, 3]).wait()

    own = rows_at(core * 4 + x, 128)
    hot_grad[own] = sums[...].reshape(128, 128)

    def spread_block(rows, to, k):
        cp = pltpu.make_async_remote_copy(
            src_ref=hot_grad.at[rows], dst_ref=hot_grad.at[rows], send_sem=sem_d.at[0, k],
            recv_sem=sem_d.at[1, k], device_id=to, device_id_type=MESH,
        )
        cp.start()
        return cp

    d_copies = [spread_block(own, near(ox), ox - 1) for ox in (1, 2, 3)]
    forwards = [spread_block(own, sibling, 3)]
    for ox in (1, 3, 2):
        d_copies[ox - 1].wait_recv()
        forwards.append(spread_block(rows_at(core * 4 + (x + 4 - ox) % 4, 128), sibling, 3 + ox))

    wait_all(outgoing, arrived, 4)
    cold_grad[...] = joined(mm(chosen_t, halves(arrived[...].reshape(512, 128))))
    for cp in forwards:
        cp.wait_recv()

    for cp in [c for cs in weight_copies.values() for c in cs] + weight_hands + pool_copies + bag_copies + a_copies + d_copies + forwards:
        cp.wait_send()
    wait_sent(req, 0)
    wait_sent(rows_out, 1)
    wait_sent(outgoing, 4)
    pltpu.make_async_copy(acc.at[pl.ds(0, 63)], acc.at[pl.ds(0, 63)], sem_x.at[0, 2]).wait()
    pltpu.make_async_copy(sums.at[pl.ds(0, 63)], sums.at[pl.ds(0, 63)], sem_x.at[0, 3]).wait()


def per_device(
    hot_ids, touched, cold_items, bag_counts, owner_map, grad_out, weight_in, bias_in, weight_out,
    hot_table, hot_accum, cold_table, cold_accum,
):
    vmem = pl.BlockSpec(memory_space=pltpu.VMEM)
    v = pltpu.VMEM
    dma = pltpu.SemaphoreType.DMA
    hot_grad, cold_grad = pl.pallas_call(
        step_kernel,
        out_shape=(v((1024, 128), F32), v((256, 128), F32)),
        in_specs=[vmem] * 4 + [pl.BlockSpec(memory_space=pl.ANY)] * 7,
        out_specs=(vmem, vmem),
        scratch_shapes=[
            v((1024, 512), BF16), v((512, 256), BF16), v((1, 512), F32),
            v((128, 1, 128), F32), v((128, 1, 128), F32),
            v((128, 4, 128), F32), v((128, 4, 128), F32),
            v((1024, 2048), BF16), v((256, 2048), BF16), v((1024, 512), BF16), v((512, 1024), BF16),
            v((1024, 1792), BF16), v((256, 896), BF16), v((256, 512), F32), v((256, 512), F32),
            v((1024, 128), BF16), v((3, 256, 128), BF16), v((4, 256, 128), F32),
            v((1024, 128), F32), v((7, 128, 128), F32), v((64, 2, 128), F32), v((64, 2, 128), F32),
            v((64, 2, 128), F32),
            v((128, 4, 128), F32), v((128, 4, 128), F32),
            v((1024, 128), F32), v((256, 128), F32), v((256, 256), BF16), v((1024, 128), I32), dma((7,)), dma((2, 6)),
            dma((2, 9)), dma((2, 3)), dma((2, 3)), dma((2, 7)), dma((2, 7)), dma((2, 5)),
        ],
        compiler_params=pltpu.CompilerParams(
            collective_id=0, has_side_effects=True, vmem_limit_bytes=56 << 20
        ),
        name="step",
    )(
        hot_ids.T, touched, cold_items, bag_counts, owner_map.reshape(1024, 128), grad_out, weight_in,
        bias_in.reshape(1, 128), weight_out, hot_table, cold_table,
    )
    return pl.pallas_call(
        adagrad_kernel,
        out_shape=tuple(jax.ShapeDtypeStruct(r.shape, F32) for r in (hot_table, hot_accum, cold_table, cold_accum)),
        in_specs=[vmem] * 6,
        out_specs=(vmem,) * 4,
        compiler_params=pltpu.CompilerParams(vmem_limit_bytes=16 << 20),
        name="adagrad",
    )(hot_grad, cold_grad, hot_table, hot_accum, cold_table, cold_accum)


def solution(mesh):
    return jax.shard_map(
        per_device,
        mesh=mesh,
        in_specs=(
            P("dp", None),
            P("dp", "mp", None),
            P("dp", "mp", None),
            P("dp", "mp", None),
            P(),
            P("dp", None),
            P(None, "mp"),
            P("mp"),
            P("mp", None),
            P(),
            P(),
            P(("dp", "mp"), None),
            P(("dp", "mp"), None),
        ),
        out_specs=(P(), P(), P(("dp", "mp"), None), P(("dp", "mp"), None)),
        check_vma=False,
    )
```

```python
import functools

import jax
import jax.numpy as jnp
from jax import lax
from jax.experimental import pallas as pl
from jax.experimental.pallas import tpu as pltpu
from jax.sharding import PartitionSpec as P

STEP_SIZE = 0.5
MESH = pl.DeviceIdType.MESH
F32, BF16, I32 = jnp.float32, jnp.bfloat16, jnp.int32
NT = (((1,), (1,)), ((), ()))


def adagrad_kernel(hot_grad, cold_grad, hot, hot_acc, cold, cold_acc, hot_new, hot_acc_new, cold_new, cold_acc_new):
    for grad, table, accum, table_new, accum_new in (
        (hot_grad, hot, hot_acc, hot_new, hot_acc_new),
        (cold_grad, cold, cold_acc, cold_new, cold_acc_new),
    ):
        g = grad[...]
        a = accum[...] + g * g
        accum_new[...] = a
        table_new[...] = table[...] - STEP_SIZE * g * lax.rsqrt(a)


def iota(shape, dim):
    return lax.broadcasted_iota(I32, shape, dim)


def mm(a, b):
    return jnp.dot(a, b, preferred_element_type=F32)


def mm_nt(a, b):
    return lax.dot_general(a, b, NT, preferred_element_type=F32)


def ones_where(mask):
    return jnp.where(mask, 1.0, 0.0).astype(BF16)


def halves(x):
    high = x.astype(BF16)
    low = (x - high.astype(F32)).astype(BF16)
    return jnp.concatenate([high, low], axis=1)


def joined(x):
    half = x.shape[1] // 2
    return x[:, :half] + x[:, half:]


def column(row):
    parts = [
        jnp.broadcast_to(row[:, k : k + 128], (128, 128)).T for k in range(0, row.shape[1], 128)
    ]
    return parts[0] if len(parts) == 1 else jnp.concatenate(parts, axis=0)


def rows_at(index, size):
    return pl.ds(pl.multiple_of(index * size, size), size)


def step_kernel(
    ids_ref, touched_ref, items_ref, counts_ref, owner_ref, grad_ref, win_ref, bias_ref, wout_ref,
    hot_ref, cold_ref, hot_grad, cold_grad,
    full_in, full_out, full_bias, req, asked, rows_out, rows_back, member, picks, bag_mat, bag_mat_t,
    gather_t, hot_in, hot_pre, back, pooled, pool_in, bag, part, part_in, acc, acc_in, sums, outgoing,
    arrived, hot_own, cold_own, grad_own, sem_l, sem_w, sem_pool, sem_bag, sem_a, sem_d, sem_x,
):
    dp, x = lax.axis_index("dp"), lax.axis_index("mp")
    core = dp % 2
    plane = dp // 2

    def near(ox):
        return (dp, (x + ox) % 4)

    barrier = pltpu.get_barrier_semaphore()
    for ox in range(1, 4):
        pl.semaphore_signal(barrier, inc=1, device_id=near(ox), device_id_type=MESH)

    for o in range(1, 128):
        pl.semaphore_signal(barrier, inc=1, device_id=((dp + o) % 128, x), device_id_type=MESH)

    share = rows_at(x, 256)
    mine = rows_at(x, 128)
    local = [
        pltpu.make_async_copy(src, dst, sem_l.at[k])
        for k, (src, dst) in enumerate((
            (cold_ref, cold_own), (win_ref, full_in.at[:, mine]), (wout_ref, full_out.at[mine]),
            (bias_ref, full_bias.at[:, mine]), (hot_ref, hot_own), (grad_ref.at[share], grad_own),
        ))
    ]
    for cp in local:
        cp.start()

    touched = column(touched_ref[0].astype(F32)).astype(I32)
    lane = iota((256, 128), 1)
    owner_row = touched >> 7
    picked = jnp.concatenate(
        [ones_where(owner_row == lane + 128 * k) for k in range(8)], axis=1
    )
    owners = owner_ref[...]
    tables = jnp.concatenate(
        [(owners >> 10).astype(F32).astype(BF16), (owners & 255).astype(F32).astype(BF16)], axis=1
    )
    found = mm(picked, tables)
    here = (touched & 127) == lane
    owner = jnp.sum(jnp.where(here, found[:, :128], 0.0), axis=1, keepdims=True)
    slot = jnp.sum(jnp.where(here, found[:, 128:], 0.0), axis=1, keepdims=True)
    lane_f = lane.astype(F32)
    hits = jnp.where(owner == lane_f, 1.0, 0.0)
    earlier = ones_where(iota((256, 256), 0) > iota((256, 256), 1))
    rank = jnp.sum(mm(earlier, hits.astype(BF16)) * hits, axis=1, keepdims=True)
    ranked = jnp.where(rank == lane_f, slot + 1.0, 0.0).astype(BF16)
    req[:, 0, :] = mm(hits.T.astype(BF16), ranked)
    bucket = owner * 4.0 + rank

    pl.semaphore_wait(barrier, 130)

    def send_all(src, dst, k):
        for o in range(1, 128):
            to = (dp + o) % 128
            pltpu.make_async_remote_copy(
                src_ref=src.at[to], dst_ref=dst.at[dp], send_sem=sem_x.at[0, k], recv_sem=sem_x.at[1, k],
                device_id=(to, x), device_id_type=MESH,
            ).start()
        dst[dp] = src[dp]

    def wait_all(src, dst, k):
        some = dst.at[pl.ds(0, 127)]
        pltpu.make_async_copy(some, some, sem_x.at[1, k]).wait()

    def wait_sent(src, k):
        some = src.at[pl.ds(0, 127)]
        pltpu.make_async_copy(some, some, sem_x.at[0, k]).wait()

    def to_near(ox, src, dst, sems, k):
        cp = pltpu.make_async_remote_copy(
            src_ref=src, dst_ref=dst, send_sem=sems.at[0, k], recv_sem=sems.at[1, k],
            device_id=near(ox), device_id_type=MESH,
        )
        cp.start()
        return cp

    send_all(req, asked, 0)

    weight_copies = []
    for ox in range(1, 4):
        weight_copies.append(to_near(ox, win_ref, full_in.at[:, mine], sem_w, ox - 1))
        weight_copies.append(to_near(ox, wout_ref, full_out.at[mine], sem_w, ox + 2))
        weight_copies.append(to_near(ox, bias_ref, full_bias.at[:, mine], sem_w, ox + 5))

    counts = counts_ref[0].astype(F32)
    eight = jnp.concatenate([counts[:, 128 * j : 128 * (j + 1)] for j in range(8)], axis=0)
    upto = ones_where(iota((128, 128), 0) <= iota((128, 128), 1))
    ends = mm(eight.astype(BF16), upto)
    total = jnp.zeros((1, 1), F32)
    item_pos = iota((128, 2048), 1).astype(F32)
    for j in range(8):
        end = ends[j : j + 1] + total
        total = end[:, 127:128]
        end_col = column(end)[:, :1]
        start_col = column(end - eight[j : j + 1])[:, :1]
        member[128 * j : 128 * (j + 1)] = ones_where((item_pos >= start_col) & (item_pos < end_col))
    picks[...] = ones_where(items_ref[0] == iota((256, 2048), 0))
    local[0].wait()
    cold_halves = halves(cold_own[...])

    wait_all(req, asked, 0)

    wanted = asked[:, 0, :].astype(BF16)
    spread = mm(ones_where((iota((512, 128), 0) >> 2) == iota((512, 128), 1)), wanted)
    wanted_col = jnp.sum(
        jnp.where((iota((512, 128), 0) & 3) == iota((512, 128), 1), spread, 0.0), axis=1, keepdims=True
    )
    chosen = ones_where(wanted_col == (iota((512, 256), 1) + 1).astype(F32))
    rows_out[...] = joined(mm(chosen, cold_halves)).reshape(128, 4, 128)
    send_all(rows_out, rows_back, 1)

    count_mat = mm_nt(member[...], picks[...]).astype(BF16)
    spot = jnp.where(bucket == iota((256, 512), 1).astype(F32), 1.0, 0.0)
    bag_mat[...] = mm(count_mat, spot.astype(BF16)).astype(BF16)
    count_mat_t = mm_nt(picks[...], member[...]).astype(BF16)
    bag_mat_t[...] = mm(spot.T.astype(BF16), count_mat_t).astype(BF16)

    for cp in local[1:]:
        cp.wait()
    ids = ids_ref[:, share]
    hot_bf = hot_own[...].astype(BF16)
    row_of = iota((1024, 256), 0)
    lane_1k = iota((256, 1024), 1).astype(F32)
    for f in range(7):
        one = ids[f : f + 1]
        gather_t[:, 256 * f : 256 * (f + 1)] = ones_where(row_of == one)
        pick_f = ones_where(column(one.astype(F32))[:, :1] == lane_1k)
        hot_in[:, 128 * f : 128 * (f + 1)] = mm(pick_f, hot_bf).astype(BF16)
    for cp in weight_copies:
        cp.wait_recv()
    hot_pre[...] = mm(hot_in[...], full_in[0:896]) + full_bias[...]
    back[...] = mm_nt(grad_own[...], full_out[...])

    wait_all(rows_out, rows_back, 1)
    rows = halves(rows_back[...].reshape(512, 128))
    pool_copies = []
    for ox in (2, 1, 3):
        there = rows_at((x + ox) % 4, 256)
        pooled[there] = joined(mm(bag_mat[there], rows)).astype(BF16)
        pool_copies.append(to_near(ox, pooled.at[there], pool_in.at[ox - 1], sem_pool, ox - 1))
    pool_sum = joined(mm(bag_mat[share], rows))
    for cp in pool_copies:
        cp.wait_recv()
    for k in range(3):
        pool_sum = pool_sum + pool_in[k].astype(F32)

    pre = hot_pre[...] + mm(pool_sum.astype(BF16), full_in[896:1024])
    gate = jax.nn.sigmoid(pre)
    hidden = (back[...] * gate * (1.0 + pre * (1.0 - gate))).astype(BF16)
    bag[x] = mm_nt(hidden, full_in[896:1024])
    in_grad = jnp.concatenate(
        [halves(mm_nt(hidden, full_in[128 * f : 128 * (f + 1)])) for f in range(7)], axis=0
    )

    a_copies = []
    for oc, ox in ((1, 2), (0, 2), (1, 1), (1, 3), (0, 1), (0, 3), (1, 0), (0, 0)):
        there = rows_at(((core + oc) % 2) * 4 + (x + ox) % 4, 128)
        part[there] = joined(mm(gather_t[there], in_grad))
        k = oc * 4 + ox
        if k:
            cp = pltpu.make_async_remote_copy(
                src_ref=part.at[there], dst_ref=part_in.at[k - 1], send_sem=sem_a.at[0, k - 1],
                recv_sem=sem_a.at[1, k - 1], device_id=(plane * 2 + (core + oc) % 2, (x + ox) % 4),
                device_id_type=MESH,
            )
            cp.start()
            a_copies.append(cp)
    bag_copies = [to_near(ox, bag.at[x], bag.at[x], sem_bag, ox - 1) for ox in (2, 1, 3)]
    for cp in a_copies:
        cp.wait_recv()
    block = part[rows_at(core * 4 + x, 128)]
    for k in range(7):
        block = block + part_in[k]
    acc[...] = block.reshape(64, 2, 128)

    for o in range(1, 64):
        to = (plane + o) % 64
        pltpu.make_async_remote_copy(
            src_ref=acc.at[to], dst_ref=acc_in.at[plane], send_sem=sem_x.at[0, 2], recv_sem=sem_x.at[1, 2],
            device_id=(to * 2 + core, x), device_id_type=MESH,
        ).start()

    acc_in[plane] = acc[plane]

    pltpu.make_async_copy(acc_in.at[pl.ds(0, 63)], acc_in.at[pl.ds(0, 63)], sem_x.at[1, 2]).wait()
    sums[plane] = jnp.sum(acc_in[...], axis=0)

    for o in range(1, 64):
        to = (plane + o) % 64
        pltpu.make_async_remote_copy(
            src_ref=sums.at[plane], dst_ref=sums.at[plane], send_sem=sem_x.at[0, 3], recv_sem=sem_x.at[1, 3],
            device_id=(to * 2 + core, x), device_id_type=MESH,
        ).start()

    for cp in bag_copies:
        cp.wait_recv()
    bag_all = halves(bag[...].reshape(1024, 128))
    outgoing[...] = joined(mm(bag_mat_t[...], bag_all)).reshape(128, 4, 128)

    send_all(outgoing, arrived, 4)
    wanted_rows = jnp.broadcast_to(wanted_col, (512, 128)).T[0:1]
    chosen_t = ones_where(wanted_rows == (iota((256, 512), 0) + 1).astype(F32))
    pltpu.make_async_copy(sums.at[pl.ds(0, 63)], sums.at[pl.ds(0, 63)], sem_x.at[1, 3]).wait()

    own = rows_at(core * 4 + x, 128)
    hot_grad[own] = sums[...].reshape(128, 128)

    def spread_block(rows, to, k):
        cp = pltpu.make_async_remote_copy(
            src_ref=hot_grad.at[rows], dst_ref=hot_grad.at[rows], send_sem=sem_d.at[0, k],
            recv_sem=sem_d.at[1, k], device_id=to, device_id_type=MESH,
        )
        cp.start()
        return cp

    sibling = (plane * 2 + 1 - core, x)
    d_copies = [spread_block(own, near(ox), ox - 1) for ox in (1, 2, 3)]
    forwards = [spread_block(own, sibling, 3)]
    for ox in (1, 3, 2):
        d_copies[ox - 1].wait_recv()
        forwards.append(spread_block(rows_at(core * 4 + (x + 4 - ox) % 4, 128), sibling, 3 + ox))

    wait_all(outgoing, arrived, 4)
    cold_grad[...] = joined(mm(chosen_t, halves(arrived[...].reshape(512, 128))))
    for cp in forwards:
        cp.wait_recv()

    for cp in weight_copies + pool_copies + bag_copies + a_copies + d_copies + forwards:
        cp.wait_send()
    wait_sent(req, 0)
    wait_sent(rows_out, 1)
    wait_sent(outgoing, 4)
    pltpu.make_async_copy(acc.at[pl.ds(0, 63)], acc.at[pl.ds(0, 63)], sem_x.at[0, 2]).wait()
    pltpu.make_async_copy(sums.at[pl.ds(0, 63)], sums.at[pl.ds(0, 63)], sem_x.at[0, 3]).wait()


def per_device(
    hot_ids, touched, cold_items, bag_counts, owner_map, grad_out, weight_in, bias_in, weight_out,
    hot_table, hot_accum, cold_table, cold_accum,
):
    vmem = pl.BlockSpec(memory_space=pltpu.VMEM)
    v = pltpu.VMEM
    dma = pltpu.SemaphoreType.DMA
    hot_grad, cold_grad = pl.pallas_call(
        step_kernel,
        out_shape=(v((1024, 128), F32), v((256, 128), F32)),
        in_specs=[vmem] * 5 + [pl.BlockSpec(memory_space=pl.ANY)] * 6,
        out_specs=(vmem, vmem),
        scratch_shapes=[
            v((1024, 512), BF16), v((512, 256), BF16), v((1, 512), F32),
            v((128, 1, 128), F32), v((128, 1, 128), F32),
            v((128, 4, 128), F32), v((128, 4, 128), F32),
            v((1024, 2048), BF16), v((256, 2048), BF16), v((1024, 512), BF16), v((512, 1024), BF16),
            v((1024, 1792), BF16), v((256, 896), BF16), v((256, 512), F32), v((256, 512), F32),
            v((1024, 128), BF16), v((3, 256, 128), BF16), v((4, 256, 128), F32),
            v((1024, 128), F32), v((7, 128, 128), F32), v((64, 2, 128), F32), v((64, 2, 128), F32),
            v((64, 2, 128), F32),
            v((128, 4, 128), F32), v((128, 4, 128), F32),
            v((1024, 128), F32), v((256, 128), F32), v((256, 256), BF16), dma((6,)),
            dma((2, 9)), dma((2, 3)), dma((2, 3)), dma((2, 7)), dma((2, 7)), dma((2, 5)),
        ],
        compiler_params=pltpu.CompilerParams(
            collective_id=0, has_side_effects=True, vmem_limit_bytes=56 << 20
        ),
        name="step",
    )(
        hot_ids.T, touched, cold_items, bag_counts, owner_map.reshape(1024, 128), grad_out, weight_in,
        bias_in.reshape(1, 128), weight_out, hot_table, cold_table,
    )
    return pl.pallas_call(
        adagrad_kernel,
        out_shape=tuple(jax.ShapeDtypeStruct(r.shape, F32) for r in (hot_table, hot_accum, cold_table, cold_accum)),
        in_specs=[vmem] * 6,
        out_specs=(vmem,) * 4,
        compiler_params=pltpu.CompilerParams(vmem_limit_bytes=16 << 20),
        name="adagrad",
    )(hot_grad, cold_grad, hot_table, hot_accum, cold_table, cold_accum)


def solution(mesh):
    return jax.shard_map(
        per_device,
        mesh=mesh,
        in_specs=(
            P("dp", None),
            P("dp", "mp", None),
            P("dp", "mp", None),
            P("dp", "mp", None),
            P(),
            P("dp", None),
            P(None, "mp"),
            P("mp"),
            P("mp", None),
            P(),
            P(),
            P(("dp", "mp"), None),
            P(("dp", "mp"), None),
        ),
        out_specs=(P(), P(), P(("dp", "mp"), None), P(("dp", "mp"), None)),
        check_vma=False,
    )
```

```python
import functools

import jax
import jax.numpy as jnp
from jax import lax
from jax.experimental import pallas as pl
from jax.experimental.pallas import tpu as pltpu
from jax.sharding import PartitionSpec as P

STEP_SIZE = 0.5
MESH = pl.DeviceIdType.MESH
F32, BF16, I32 = jnp.float32, jnp.bfloat16, jnp.int32
NT = (((1,), (1,)), ((), ()))


def adagrad_kernel(hot_grad, cold_grad, hot, hot_acc, cold, cold_acc, hot_new, hot_acc_new, cold_new, cold_acc_new):
    for grad, table, accum, table_new, accum_new in (
        (hot_grad, hot, hot_acc, hot_new, hot_acc_new),
        (cold_grad, cold, cold_acc, cold_new, cold_acc_new),
    ):
        g = grad[...]
        a = accum[...] + g * g
        accum_new[...] = a
        table_new[...] = table[...] - STEP_SIZE * g * lax.rsqrt(a)


def iota(shape, dim):
    return lax.broadcasted_iota(I32, shape, dim)


def mm(a, b):
    return jnp.dot(a, b, preferred_element_type=F32)


def mm_nt(a, b):
    return lax.dot_general(a, b, NT, preferred_element_type=F32)


def ones_where(mask):
    return jnp.where(mask, 1.0, 0.0).astype(BF16)


def halves(x):
    high = x.astype(BF16)
    low = (x - high.astype(F32)).astype(BF16)
    return jnp.concatenate([high, low], axis=1)


def joined(x):
    half = x.shape[1] // 2
    return x[:, :half] + x[:, half:]


def column(row):
    parts = [
        jnp.broadcast_to(row[:, k : k + 128], (128, 128)).T for k in range(0, row.shape[1], 128)
    ]
    return parts[0] if len(parts) == 1 else jnp.concatenate(parts, axis=0)


def rows_at(index, size):
    return pl.ds(pl.multiple_of(index * size, size), size)


def step_kernel(
    ids_ref, touched_ref, items_ref, counts_ref, owner_ref, grad_ref, win_ref, bias_ref, wout_ref,
    hot_ref, cold_ref, hot_grad, cold_grad,
    full_in, full_out, full_bias, req, asked, rows_out, rows_back, member, picks, bag_mat, bag_mat_t,
    gather_t, hot_in, hot_pre, back, pooled, pool_in, bag, part, part_in, acc, acc_in, sums, outgoing,
    arrived, hot_own, cold_own, grad_own, sem_l, sem_w, sem_pool, sem_bag, sem_a, sem_d, sem_x,
):
    dp, x = lax.axis_index("dp"), lax.axis_index("mp")
    core = dp % 2
    plane = dp // 2

    def near(ox):
        return (dp, (x + ox) % 4)

    barrier = pltpu.get_barrier_semaphore()
    for ox in range(1, 4):
        pl.semaphore_signal(barrier, inc=1, device_id=near(ox), device_id_type=MESH)

    for o in range(1, 128):
        pl.semaphore_signal(barrier, inc=1, device_id=((dp + o) % 128, x), device_id_type=MESH)

    share = rows_at(x, 256)
    mine = rows_at(x, 128)
    local = [
        pltpu.make_async_copy(src, dst, sem_l.at[k])
        for k, (src, dst) in enumerate((
            (cold_ref, cold_own), (win_ref, full_in.at[:, mine]), (wout_ref, full_out.at[mine]),
            (bias_ref, full_bias.at[:, mine]), (hot_ref, hot_own), (grad_ref.at[share], grad_own),
        ))
    ]
    for cp in local:
        cp.start()

    touched = column(touched_ref[0].astype(F32)).astype(I32)
    lane = iota((256, 128), 1)
    owner_row = touched >> 7
    picked = jnp.concatenate(
        [ones_where(owner_row == lane + 128 * k) for k in range(8)], axis=1
    )
    owners = owner_ref[...]
    tables = jnp.concatenate(
        [(owners >> 10).astype(F32).astype(BF16), (owners & 255).astype(F32).astype(BF16)], axis=1
    )
    found = mm(picked, tables)
    here = (touched & 127) == lane
    owner = jnp.sum(jnp.where(here, found[:, :128], 0.0), axis=1, keepdims=True)
    slot = jnp.sum(jnp.where(here, found[:, 128:], 0.0), axis=1, keepdims=True)
    lane_f = lane.astype(F32)
    hits = jnp.where(owner == lane_f, 1.0, 0.0)
    earlier = ones_where(iota((256, 256), 0) > iota((256, 256), 1))
    rank = jnp.sum(mm(earlier, hits.astype(BF16)) * hits, axis=1, keepdims=True)
    ranked = jnp.where(rank == lane_f, slot + 1.0, 0.0).astype(BF16)
    req[:, 0, :] = mm(hits.T.astype(BF16), ranked)
    bucket = owner * 4.0 + rank

    pl.semaphore_wait(barrier, 130)

    def send_all(src, dst, k):
        @pl.loop(1, 128)
        def _(o):
            to = (dp + o) % 128
            pltpu.make_async_remote_copy(
                src_ref=src.at[to], dst_ref=dst.at[dp], send_sem=sem_x.at[0, k], recv_sem=sem_x.at[1, k],
                device_id=(to, x), device_id_type=MESH,
            ).start()
        dst[dp] = src[dp]

    def wait_all(src, dst, k):
        some = dst.at[pl.ds(0, 127)]
        pltpu.make_async_copy(some, some, sem_x.at[1, k]).wait()

    def wait_sent(src, k):
        some = src.at[pl.ds(0, 127)]
        pltpu.make_async_copy(some, some, sem_x.at[0, k]).wait()

    def to_near(ox, src, dst, sems, k):
        cp = pltpu.make_async_remote_copy(
            src_ref=src, dst_ref=dst, send_sem=sems.at[0, k], recv_sem=sems.at[1, k],
            device_id=near(ox), device_id_type=MESH,
        )
        cp.start()
        return cp

    send_all(req, asked, 0)

    weight_copies = []
    for ox in range(1, 4):
        weight_copies.append(to_near(ox, win_ref, full_in.at[:, mine], sem_w, ox - 1))
        weight_copies.append(to_near(ox, wout_ref, full_out.at[mine], sem_w, ox + 2))
        weight_copies.append(to_near(ox, bias_ref, full_bias.at[:, mine], sem_w, ox + 5))

    counts = counts_ref[0].astype(F32)
    eight = jnp.concatenate([counts[:, 128 * j : 128 * (j + 1)] for j in range(8)], axis=0)
    upto = ones_where(iota((128, 128), 0) <= iota((128, 128), 1))
    ends = mm(eight.astype(BF16), upto)
    total = jnp.zeros((1, 1), F32)
    item_pos = iota((128, 2048), 1).astype(F32)
    for j in range(8):
        end = ends[j : j + 1] + total
        total = end[:, 127:128]
        end_col = column(end)[:, :1]
        start_col = column(end - eight[j : j + 1])[:, :1]
        member[128 * j : 128 * (j + 1)] = ones_where((item_pos >= start_col) & (item_pos < end_col))
    picks[...] = ones_where(items_ref[0] == iota((256, 2048), 0))
    local[0].wait()
    cold_halves = halves(cold_own[...])

    wait_all(req, asked, 0)

    wanted = asked[:, 0, :].astype(BF16)
    spread = mm(ones_where((iota((512, 128), 0) >> 2) == iota((512, 128), 1)), wanted)
    wanted_col = jnp.sum(
        jnp.where((iota((512, 128), 0) & 3) == iota((512, 128), 1), spread, 0.0), axis=1, keepdims=True
    )
    chosen = ones_where(wanted_col == (iota((512, 256), 1) + 1).astype(F32))
    rows_out[...] = joined(mm(chosen, cold_halves)).reshape(128, 4, 128)
    send_all(rows_out, rows_back, 1)

    count_mat = mm_nt(member[...], picks[...]).astype(BF16)
    spot = jnp.where(bucket == iota((256, 512), 1).astype(F32), 1.0, 0.0)
    bag_mat[...] = mm(count_mat, spot.astype(BF16)).astype(BF16)
    count_mat_t = mm_nt(picks[...], member[...]).astype(BF16)
    bag_mat_t[...] = mm(spot.T.astype(BF16), count_mat_t).astype(BF16)

    for cp in local[1:]:
        cp.wait()
    ids = ids_ref[:, share]
    hot_bf = hot_own[...].astype(BF16)
    row_of = iota((1024, 256), 0)
    lane_1k = iota((256, 1024), 1).astype(F32)
    for f in range(7):
        one = ids[f : f + 1]
        gather_t[:, 256 * f : 256 * (f + 1)] = ones_where(row_of == one)
        pick_f = ones_where(column(one.astype(F32))[:, :1] == lane_1k)
        hot_in[:, 128 * f : 128 * (f + 1)] = mm(pick_f, hot_bf).astype(BF16)
    for cp in weight_copies:
        cp.wait_recv()
    hot_pre[...] = mm(hot_in[...], full_in[0:896]) + full_bias[...]
    back[...] = mm_nt(grad_own[...], full_out[...])

    wait_all(rows_out, rows_back, 1)
    rows = halves(rows_back[...].reshape(512, 128))
    pool_copies = []
    for ox in (2, 1, 3):
        there = rows_at((x + ox) % 4, 256)
        pooled[there] = joined(mm(bag_mat[there], rows)).astype(BF16)
        pool_copies.append(to_near(ox, pooled.at[there], pool_in.at[ox - 1], sem_pool, ox - 1))
    pool_sum = joined(mm(bag_mat[share], rows))
    for cp in pool_copies:
        cp.wait_recv()
    for k in range(3):
        pool_sum = pool_sum + pool_in[k].astype(F32)

    pre = hot_pre[...] + mm(pool_sum.astype(BF16), full_in[896:1024])
    gate = jax.nn.sigmoid(pre)
    hidden = (back[...] * gate * (1.0 + pre * (1.0 - gate))).astype(BF16)
    bag[x] = mm_nt(hidden, full_in[896:1024])
    in_grad = jnp.concatenate(
        [halves(mm_nt(hidden, full_in[128 * f : 128 * (f + 1)])) for f in range(7)], axis=0
    )

    a_copies = []
    for oc, ox in ((1, 2), (0, 2), (1, 1), (1, 3), (0, 1), (0, 3), (1, 0), (0, 0)):
        there = rows_at(((core + oc) % 2) * 4 + (x + ox) % 4, 128)
        part[there] = joined(mm(gather_t[there], in_grad))
        k = oc * 4 + ox
        if k:
            cp = pltpu.make_async_remote_copy(
                src_ref=part.at[there], dst_ref=part_in.at[k - 1], send_sem=sem_a.at[0, k - 1],
                recv_sem=sem_a.at[1, k - 1], device_id=(plane * 2 + (core + oc) % 2, (x + ox) % 4),
                device_id_type=MESH,
            )
            cp.start()
            a_copies.append(cp)
    bag_copies = [to_near(ox, bag.at[x], bag.at[x], sem_bag, ox - 1) for ox in (2, 1, 3)]
    for cp in a_copies:
        cp.wait_recv()
    block = part[rows_at(core * 4 + x, 128)]
    for k in range(7):
        block = block + part_in[k]
    acc[...] = block.reshape(64, 2, 128)

    @pl.loop(1, 64)
    def _(o):
        to = (plane + o) % 64
        pltpu.make_async_remote_copy(
            src_ref=acc.at[to], dst_ref=acc_in.at[plane], send_sem=sem_x.at[0, 2], recv_sem=sem_x.at[1, 2],
            device_id=(to * 2 + core, x), device_id_type=MESH,
        ).start()

    acc_in[plane] = acc[plane]

    for cp in bag_copies:
        cp.wait_recv()
    bag_all = halves(bag[...].reshape(1024, 128))
    outgoing[...] = joined(mm(bag_mat_t[...], bag_all)).reshape(128, 4, 128)

    pltpu.make_async_copy(acc_in.at[pl.ds(0, 63)], acc_in.at[pl.ds(0, 63)], sem_x.at[1, 2]).wait()
    sums[plane] = jnp.sum(acc_in[...], axis=0)

    @pl.loop(1, 64)
    def _(o):
        to = (plane + o) % 64
        pltpu.make_async_remote_copy(
            src_ref=sums.at[plane], dst_ref=sums.at[plane], send_sem=sem_x.at[0, 3], recv_sem=sem_x.at[1, 3],
            device_id=(to * 2 + core, x), device_id_type=MESH,
        ).start()

    send_all(outgoing, arrived, 4)
    wanted_rows = jnp.broadcast_to(wanted_col, (512, 128)).T[0:1]
    chosen_t = ones_where(wanted_rows == (iota((256, 512), 0) + 1).astype(F32))
    pltpu.make_async_copy(sums.at[pl.ds(0, 63)], sums.at[pl.ds(0, 63)], sem_x.at[1, 3]).wait()

    own = rows_at(core * 4 + x, 128)
    hot_grad[own] = sums[...].reshape(128, 128)

    def spread_block(rows, to, k):
        cp = pltpu.make_async_remote_copy(
            src_ref=hot_grad.at[rows], dst_ref=hot_grad.at[rows], send_sem=sem_d.at[0, k],
            recv_sem=sem_d.at[1, k], device_id=to, device_id_type=MESH,
        )
        cp.start()
        return cp

    sibling = (plane * 2 + 1 - core, x)
    d_copies = [spread_block(own, near(ox), ox - 1) for ox in (1, 2, 3)]
    forwards = [spread_block(own, sibling, 3)]
    for ox in (1, 3, 2):
        d_copies[ox - 1].wait_recv()
        forwards.append(spread_block(rows_at(core * 4 + (x + 4 - ox) % 4, 128), sibling, 3 + ox))

    wait_all(outgoing, arrived, 4)
    cold_grad[...] = joined(mm(chosen_t, halves(arrived[...].reshape(512, 128))))
    for cp in forwards:
        cp.wait_recv()

    for cp in weight_copies + pool_copies + bag_copies + a_copies + d_copies + forwards:
        cp.wait_send()
    wait_sent(req, 0)
    wait_sent(rows_out, 1)
    wait_sent(outgoing, 4)
    pltpu.make_async_copy(acc.at[pl.ds(0, 63)], acc.at[pl.ds(0, 63)], sem_x.at[0, 2]).wait()
    pltpu.make_async_copy(sums.at[pl.ds(0, 63)], sums.at[pl.ds(0, 63)], sem_x.at[0, 3]).wait()


def per_device(
    hot_ids, touched, cold_items, bag_counts, owner_map, grad_out, weight_in, bias_in, weight_out,
    hot_table, hot_accum, cold_table, cold_accum,
):
    vmem = pl.BlockSpec(memory_space=pltpu.VMEM)
    v = pltpu.VMEM
    dma = pltpu.SemaphoreType.DMA
    hot_grad, cold_grad = pl.pallas_call(
        step_kernel,
        out_shape=(v((1024, 128), F32), v((256, 128), F32)),
        in_specs=[vmem] * 5 + [pl.BlockSpec(memory_space=pl.ANY)] * 6,
        out_specs=(vmem, vmem),
        scratch_shapes=[
            v((1024, 512), BF16), v((512, 256), BF16), v((1, 512), F32),
            v((128, 1, 128), F32), v((128, 1, 128), F32),
            v((128, 4, 128), F32), v((128, 4, 128), F32),
            v((1024, 2048), BF16), v((256, 2048), BF16), v((1024, 512), BF16), v((512, 1024), BF16),
            v((1024, 1792), BF16), v((256, 896), BF16), v((256, 512), F32), v((256, 512), F32),
            v((1024, 128), BF16), v((3, 256, 128), BF16), v((4, 256, 128), F32),
            v((1024, 128), F32), v((7, 128, 128), F32), v((64, 2, 128), F32), v((64, 2, 128), F32),
            v((64, 2, 128), F32),
            v((128, 4, 128), F32), v((128, 4, 128), F32),
            v((1024, 128), F32), v((256, 128), F32), v((256, 256), BF16), dma((6,)),
            dma((2, 9)), dma((2, 3)), dma((2, 3)), dma((2, 7)), dma((2, 7)), dma((2, 5)),
        ],
        compiler_params=pltpu.CompilerParams(
            collective_id=0, has_side_effects=True, vmem_limit_bytes=56 << 20
        ),
        name="step",
    )(
        hot_ids.T, touched, cold_items, bag_counts, owner_map.reshape(1024, 128), grad_out, weight_in,
        bias_in.reshape(1, 128), weight_out, hot_table, cold_table,
    )
    return pl.pallas_call(
        adagrad_kernel,
        out_shape=tuple(jax.ShapeDtypeStruct(r.shape, F32) for r in (hot_table, hot_accum, cold_table, cold_accum)),
        in_specs=[vmem] * 6,
        out_specs=(vmem,) * 4,
        compiler_params=pltpu.CompilerParams(vmem_limit_bytes=16 << 20),
        name="adagrad",
    )(hot_grad, cold_grad, hot_table, hot_accum, cold_table, cold_accum)


def solution(mesh):
    return jax.shard_map(
        per_device,
        mesh=mesh,
        in_specs=(
            P("dp", None),
            P("dp", "mp", None),
            P("dp", "mp", None),
            P("dp", "mp", None),
            P(),
            P("dp", None),
            P(None, "mp"),
            P("mp"),
            P("mp", None),
            P(),
            P(),
            P(("dp", "mp"), None),
            P(("dp", "mp"), None),
        ),
        out_specs=(P(), P(), P(("dp", "mp"), None), P(("dp", "mp"), None)),
        check_vma=False,
    )
```
